256 devices in a mesh: tm: 32 (over x, z), chan: 8 (over y, core).
Axes of the slice: x: 4, y: 4, z: 8, core: 2. Of those that a mesh axis runs over, the one named last changes fastest.
Arguments:
- visibilities: bfloat16 [32, 8, 512, 1024], P('tm', None, None, 'chan'), may hold values from -6 to 6
- station_gains: float32 [8, 192, 1024], P(None, 'chan'), may hold values from -1.5 to 1.5, as said below
- station_pairs: int32 [512, 2], replicated, may hold values from 0 to 191, as said below
- average_bands: int32 [512, 2], replicated, may hold values from 0 to 3, as said below
- tile_map: int32 [512, 32], replicated, may hold values from 0 to 255
- baseline_order: int32 [512], replicated, may hold values from 0 to 511, as said below
Outputs:
- averaged: bfloat16 [32, 8, 512, 1024], P(None, None, 'tm', 'chan')
- gridded: float32 [256, 8, 1024], P('tm', None, 'chan')
The draws below stay inside these ranges and needn't reach their ends.
Inputs may be any that keep to these rules, and one draw needn't show every extreme that they name: `station_pairs`: row b holds the two stations of baseline b, the first smaller than the second. `average_bands`: column 0 is at most 3, column 1 at most 2. In each aligned block of 16 positions k of baseline_order, the bands of the baselines baseline_order[k] are, in some order, the pairs (3 - j % (3 + 1), 2 - j % (2 + 1)) for j = 0 to 15. `baseline_order`: each baseline once. `station_gains`: diagonal Jones entries have magnitudes of order one.
All inputs are finite; a program needn't handle non-finite values.
Results may differ from the reference program's by a relative error of at most 0.019.
Values may be sent and summed in bfloat16 or wider, within the bound.
No kernel may reach another device: no remote copies, remote signals or barrier semaphores. Data moves between devices by JAX's collectives and lax.ppermute only.
A program may use at most 128 MiB of HBM per device.

```python
import math
import jax
import jax.numpy as jnp
from jax import lax

NS = 192
B_DEV = 16
TLOG = 3
CLOG = 2
NT = 32
NB = 512
NC = 1024
TILES = 256


def draw_station_gains(key, part):
    streams = jax.random.split(key, 3)
    extent = (NS, NC)
    amplitude = jax.random.uniform(streams[0], (2,) + extent, jnp.float32, 0.5, 1.5)
    leakage = jnp.clip(0.2 * jax.random.normal(streams[2], (4,) + extent, jnp.float32), -0.6, 0.6)
    phase = jax.random.uniform(streams[1], (2,) + extent, jnp.float32, -math.pi, math.pi)
    real_part = amplitude * jnp.cos(phase)
    imag_part = amplitude * jnp.sin(phase)
    return jnp.stack([real_part[0], imag_part[0], leakage[0], leakage[1], leakage[2], leakage[3], real_part[1], imag_part[1]]).astype(jnp.float32)


def draw_station_pairs(key, part):
    streams = jax.random.split(key, 2)
    first = jax.random.randint(streams[0], (NB,), 0, NS)
    offset = jax.random.randint(streams[1], (NB,), 1, NS)
    second = (first + offset) % NS
    result = jnp.stack([jnp.minimum(first, second), jnp.maximum(first, second)], axis=1)
    result = result.at[0].set(jnp.array([0, NS - 1], jnp.int32))
    return result.astype(jnp.int32)


def band_layout(key):
    base = jax.random.fold_in(key, 4099)
    streams = jax.random.split(base, 2)
    order = jax.random.permutation(streams[0], NB).astype(jnp.int32)
    block_keys = jax.random.split(streams[1], NB // B_DEV)
    slots = jax.vmap(lambda single: jax.random.permutation(single, B_DEV))(block_keys).reshape(-1).astype(jnp.int32)
    time_levels = TLOG - slots % (TLOG + 1)
    chan_levels = CLOG - slots % (CLOG + 1)
    at_position = jnp.stack([time_levels, chan_levels], axis=1).astype(jnp.int32)
    bands = jnp.zeros((NB, 2), jnp.int32).at[order].set(at_position)
    return (order, bands)


def draw_average_bands(key, part):
    order, bands = band_layout(key)
    return bands.astype(jnp.int32)


def draw_baseline_order(key, part):
    order, bands = band_layout(key)
    return order.astype(jnp.int32)


def set_ends(drawn, key, least, high):
    spot = [jax.random.randint(jax.random.fold_in(key, axis), (), 0, length) for axis, length in enumerate(drawn.shape)]
    longest = drawn.shape.index(max(drawn.shape))
    beside = spot[:longest] + [(spot[longest] + 1) % drawn.shape[longest]] + spot[longest + 1:]
    return drawn.at[tuple(spot)].set(least).at[tuple(beside)].set(high)


def levels(key, shape, shards, smallest, top_value):
    level = 1.0
    for axis_at, blocks in shards:
        heights = jax.random.uniform(jax.random.fold_in(jax.random.fold_in(key, 6), axis_at), (blocks,), jnp.float32, smallest / len(shards), top_value / len(shards))
        level = level * jnp.repeat(jnp.exp(heights), shape[axis_at] // blocks).reshape((-1,) + (1,) * (len(shape) - 1 - axis_at))
    return level


def gaussian(stream_key, shape, scale, most, pieces=(), kind=jnp.bfloat16):
    gain = levels(stream_key, shape, pieces, -0.22, 0.18) if pieces else 1.0
    drawn = jax.random.normal(stream_key, shape, jnp.float32) * scale * gain
    return jnp.minimum(jnp.maximum(drawn, -most), most).astype(kind)


def setup_inputs(seed: int = 0) -> dict:
    splits = jax.random.split(jax.random.key(seed), 7)
    visibilities = gaussian(splits[0], (NT, 8, NB, NC), 1.0, 6.0, ((0, 32), (3, 8)))
    station_gains = draw_station_gains(jax.random.fold_in(splits[6], 71), 0)
    station_pairs = draw_station_pairs(jax.random.fold_in(splits[6], 71), 0)
    average_bands = draw_average_bands(jax.random.fold_in(splits[6], 71), 0)
    tile_map = set_ends(jax.random.randint(splits[4], (NB, NT), 0, TILES), jax.random.fold_in(splits[4], 1), 0, TILES - 1).astype(jnp.int32)
    baseline_order = draw_baseline_order(jax.random.fold_in(splits[6], 71), 0)
    return {"visibilities": visibilities, "station_gains": station_gains, "station_pairs": station_pairs, "average_bands": average_bands, "tile_map": tile_map, "baseline_order": baseline_order}


def product(left, right):
    return (left[0] * right[0] - left[1] * right[1], left[0] * right[1] + left[1] * right[0])


def product_conj(left, right):
    return (left[0] * right[0] + left[1] * right[1], left[1] * right[0] - left[0] * right[1])


def add_pair(left, right):
    return (left[0] + right[0], left[1] + right[1])


def as_matrix(components):
    return [[(components[0], components[1]), (components[2], components[3])],
            [(components[4], components[5]), (components[6], components[7])]]


def jones_apply(first, middle, second):
    left_gain = as_matrix(first)
    coherency = as_matrix(middle)
    right_gain = as_matrix(second)
    partial_rows = [[add_pair(product(left_gain[i][0], coherency[0][k]), product(left_gain[i][1], coherency[1][k])) for k in range(2)] for i in range(2)]
    result = []
    for i in range(2):
        for c in range(2):
            element = add_pair(product_conj(partial_rows[i][0], right_gain[c][0]), product_conj(partial_rows[i][1], right_gain[c][1]))
            result.extend(element)
    return result


def calibrate(samples, gain_table, first_station, second_station):
    left_gain = jnp.take(gain_table, first_station, axis=1)
    right_gain = jnp.take(gain_table, second_station, axis=1)
    values = [samples[:, i].astype(jnp.float32) for i in range(8)]
    result = jones_apply([left_gain[i][None] for i in range(8)], values, [right_gain[i][None] for i in range(8)])
    return jnp.stack(result, axis=1).astype(jnp.bfloat16)


def halve_time(current, size):
    extent = current.shape[0]
    shaped = current.reshape((extent // size, 2, size // 2) + current.shape[1:])
    merged = 0.5 * (shaped[:, 0:1] + shaped[:, 1:2])
    return jnp.broadcast_to(merged, shaped.shape).reshape(current.shape)


def halve_chan(current, size):
    extent = current.shape[-1]
    shaped = current.reshape(current.shape[:-1] + (extent // size, 2, size // 2))
    merged = 0.5 * (shaped[..., 0:1, :] + shaped[..., 1:2, :])
    return jnp.broadcast_to(merged, shaped.shape).reshape(current.shape)


def band_average(samples, time_levels, chan_levels):
    values = samples.astype(jnp.float32)
    time_select = time_levels[None, None, :, None]
    chan_select = chan_levels[None, None, :, None]
    result = values
    current = values
    for k in range(1, TLOG + 1):
        current = halve_time(current, 2 ** k)
        result = jnp.where(time_select >= k, current, result)
    final = result
    current = result
    for k in range(1, CLOG + 1):
        current = halve_chan(current, 2 ** k)
        final = jnp.where(chan_select >= k, current, final)
    return final.astype(jnp.bfloat16)


def reference(visibilities, station_gains, station_pairs, average_bands, tile_map, baseline_order):
    block_count = NB // B_DEV

    def advance(uv_grid, block):
        rows_here = lax.dynamic_slice_in_dim(baseline_order, block * B_DEV, B_DEV)
        samples = jnp.take(visibilities, rows_here, axis=2)
        pairs_here = station_pairs[rows_here]
        calibrated = calibrate(samples, station_gains, pairs_here[:, 0], pairs_here[:, 1])
        bands_here = average_bands[rows_here]
        averaged = band_average(calibrated, bands_here[:, 0], bands_here[:, 1])
        tile_here = tile_map[rows_here].T
        time_index = jnp.arange(NT, dtype=jnp.int32)[:, None]
        period = jnp.left_shift(jnp.ones_like(bands_here[:, 0]), bands_here[:, 0])[None, :]
        segment = jnp.where(time_index % period == 0, tile_here, TILES)
        values = jnp.transpose(averaged.astype(jnp.float32), (0, 2, 1, 3)).reshape(NT * B_DEV, 8, NC)
        summed = jax.ops.segment_sum(values, segment.reshape(-1), num_segments=TILES + 1)
        return uv_grid + summed[:TILES], averaged

    gridded, blocks = lax.scan(advance, jnp.zeros((TILES, 8, NC), jnp.float32), jnp.arange(block_count, dtype=jnp.int32))
    averaged = jnp.moveaxis(blocks, 0, 2).reshape(NT, 8, NB, NC)
    return averaged, gridded
```

```python
import functools
import jax
import jax.numpy as jnp
from jax import lax
from jax.experimental import pallas as pl
from jax.experimental.pallas import tpu as pltpu
from jax.sharding import PartitionSpec as P

UNITS = (5, 5, 6)
BASE = (0, 5, 10)
ROW0 = (0, 40, 60)
ROWS = 72
F32 = jnp.float32
BF16 = jnp.bfloat16
VMEM_LIMIT = 24 << 20


def iota(shape, axis):
    return lax.broadcasted_iota(jnp.int32, shape, axis)


def one_hot(mask):
    return jnp.where(mask, 1.0, 0.0).astype(BF16)


def dot(a, b):
    return lax.dot_general(a, b, (((1,), (0,)), ((), ())), preferred_element_type=F32)


def dot_t(a, b):
    return lax.dot_general(a, b, (((1,), (1,)), ((), ())), preferred_element_type=F32)


def rows_of(values, width):
    row = iota((8, width), 0)
    result = jnp.zeros((8, width), F32)
    for i, value in enumerate(values):
        result = jnp.where(row == i, value, result)
    return result


def gains_kernel(gain_ref, out_ref):
    for d in range(8):
        out_ref[d] = gain_ref[:, :, d * 128 : (d + 1) * 128].astype(BF16)


def cut_gains(gains):
    comps, stations, _ = gains.shape
    return pl.pallas_call(
        gains_kernel,
        out_shape=jax.ShapeDtypeStruct((8, comps, stations, 128), BF16),
        compiler_params=pltpu.CompilerParams(vmem_limit_bytes=VMEM_LIMIT),
        name="cut_gains",
    )(gains)


def prepare_kernel(
    me_ref, pairs_ref, bands_ref, tiles_ref, order_ref, vis_ref,
    vis_out, left_out, right_out, weight_out, pick_out, lane_out, time_out,
):
    me = me_ref[0]
    nb = order_ref.shape[1]
    time_level = bands_ref[0:1, :]
    chan_level = bands_ref[1:2, :]
    tile = tiles_ref[pl.ds(me, 1), :]
    for level in range(1, 4):
        start = (me >> level) << level
        tile = jnp.where(time_level == level, tiles_ref[pl.ds(start, 1), :], tile)
    info = rows_of(
        [time_level.astype(F32), chan_level.astype(F32), tile.astype(F32)], nb
    ).astype(BF16)

    order_hot = one_hot(iota((nb, nb), 0) == order_ref[...])
    at_position = dot(info, order_hot)
    chan_here = at_position[1:2, :]
    same = rows_of([jnp.where(chan_here == float(level), 1.0, 0.0) for level in range(3)], nb)
    before = one_hot(
        (iota((nb, nb), 0) < iota((nb, nb), 1)) & ((iota((nb, nb), 0) >> 4) == (iota((nb, nb), 1) >> 4))
    )
    count = dot(same.astype(BF16), before)
    unit = jnp.where(
        chan_here == 0.0,
        count[0:1, :],
        jnp.where(chan_here == 1.0, BASE[1] + count[1:2, :], BASE[2] + count[2:3, :]),
    )
    block = iota((1, nb), 1) >> 4
    slot = unit.astype(jnp.int32) * 32 + block
    slot_hot = dot_t(one_hot(iota((nb, nb), 0) == slot), order_hot).astype(BF16)

    for c in range(0, 8, 2):
        both = jnp.concatenate([vis_ref[c], vis_ref[c + 1]], axis=1)
        moved = dot(slot_hot, both).astype(BF16)
        vis_out[c] = moved[:, :128]
        vis_out[c + 1] = moved[:, 128:]

    left_out[...] = dot_t(slot_hot, one_hot(iota((256, nb), 0) == pairs_ref[0:1, :])).astype(BF16)
    right_out[...] = dot_t(slot_hot, one_hot(iota((256, nb), 0) == pairs_ref[1:2, :])).astype(BF16)

    at_slot = dot_t(info, slot_hot)
    time_slot = at_slot[0:1, :]
    weight = jnp.where(
        time_slot == 0.0, 1.0, jnp.where(time_slot == 1.0, 0.5, jnp.where(time_slot == 2.0, 0.25, 0.125))
    )
    tile_slot = at_slot[2:3, :].astype(jnp.int32)
    weight_out[...] = jnp.where(iota((256, nb), 0) == tile_slot, weight, 0.0).astype(BF16)

    lane = iota((1, 128), 1)
    own = rows_of([at_position[0:1, :], chan_here, unit], nb).astype(BF16)
    own = dot(own, one_hot(iota((nb, 128), 0) == me * 16 + (iota((nb, 128), 1) & 15)))
    own_time = own[0:1, :]
    own_chan = own[1:2, :].astype(jnp.int32)
    own_unit = own[2:3, :].astype(jnp.int32)
    comp = lane >> 4
    packed_row = jnp.where(
        own_chan == 0,
        own_unit * 8 + comp,
        jnp.where(
            own_chan == 1,
            ROW0[1] + (own_unit - BASE[1]) * 4 + (comp >> 1),
            ROW0[2] + (own_unit - BASE[2]) * 2 + (comp >> 2),
        ),
    )
    part = jnp.where(own_chan == 0, 0, jnp.where(own_chan == 1, 1 + (comp & 1), 3 + (comp & 3)))
    sub = iota((128, 128), 0)
    lan = iota((128, 128), 1)
    eye = one_hot(sub == lan)
    row_hot = one_hot(sub == packed_row)
    pick_out[...] = dot_t(eye, row_hot).astype(BF16)
    part_hot = dot_t(eye, one_hot(sub == part)).astype(BF16)
    table = jnp.where(
        sub == 0,
        lan,
        jnp.where(sub <= 2, (sub - 1) * 64 + (lan >> 1), jnp.where(sub <= 6, (sub - 3) * 32 + (lan >> 2), 0)),
    )
    lane_out[...] = dot(part_hot, table.astype(F32).astype(BF16)).astype(jnp.int32)
    share = jnp.where(sub < ROW0[1], 1.0, jnp.where(sub < ROW0[2], 0.5, 0.25))
    spread = jnp.broadcast_to(own_time, (128, 128)).astype(BF16)
    time_out[...] = dot_t(row_hot, spread) * share


def prepare(me, pairs, bands, tiles, order, vis):
    nb = order.shape[1]
    vmem = pl.BlockSpec(memory_space=pltpu.VMEM)
    return pl.pallas_call(
        prepare_kernel,
        in_specs=[pl.BlockSpec(memory_space=pltpu.SMEM)] + [vmem] * 5,
        out_specs=[vmem] * 7,
        out_shape=[
            jax.ShapeDtypeStruct((8, nb, 128), BF16),
            jax.ShapeDtypeStruct((nb, 256), BF16),
            jax.ShapeDtypeStruct((nb, 256), BF16),
            jax.ShapeDtypeStruct((256, nb), BF16),
            jax.ShapeDtypeStruct((128, 128), BF16),
            jax.ShapeDtypeStruct((128, 128), jnp.int32),
            jax.ShapeDtypeStruct((128, 128), F32),
        ],
        compiler_params=pltpu.CompilerParams(vmem_limit_bytes=VMEM_LIMIT),
        cost_estimate=pl.CostEstimate(flops=2_000_000_000, bytes_accessed=4_000_000, transcendentals=0),
        name="prepare",
    )(me, pairs, bands, tiles, order, vis)


def product(left, right):
    return (left[0] * right[0] - left[1] * right[1], left[0] * right[1] + left[1] * right[0])


def product_conj(left, right):
    return (left[0] * right[0] + left[1] * right[1], left[1] * right[0] - left[0] * right[1])


def add_pair(left, right):
    return (left[0] + right[0], left[1] + right[1])


def as_matrix(components):
    return [
        [(components[0], components[1]), (components[2], components[3])],
        [(components[4], components[5]), (components[6], components[7])],
    ]


def jones_apply(first, middle, second):
    left_gain = as_matrix(first)
    coherency = as_matrix(middle)
    right_gain = as_matrix(second)
    partial_rows = [
        [
            add_pair(
                product(left_gain[i][0], coherency[0][k]), product(left_gain[i][1], coherency[1][k])
            )
            for k in range(2)
        ]
        for i in range(2)
    ]
    result = []
    for i in range(2):
        for c in range(2):
            element = add_pair(
                product_conj(partial_rows[i][0], right_gain[c][0]),
                product_conj(partial_rows[i][1], right_gain[c][1]),
            )
            result.extend(element)
    return result


def lanes(c):
    return slice(c * 128, (c + 1) * 128)


def calibrate_kernel(gain_ref, left_ref, right_ref, weight_ref, vis_ref, out_ref, gains, gl, gr, cal, wide):
    nb = left_ref.shape[0]
    stations = gain_ref.shape[2]
    for d in range(8):
        for c in range(8):
            gains[d * stations : (d + 1) * stations, lanes(c)] = gain_ref[d, c].astype(F32)
    gains[8 * stations :, :] = jnp.zeros((256 - 8 * stations, 1024), F32)
    table = gains[...].astype(BF16)
    gl[...] = dot(left_ref[...], table)
    gr[...] = dot(right_ref[...], table)

    def step(i, carry):
        rows = pl.ds(pl.multiple_of(i * 16, 16), 16)
        result = jones_apply(
            [gl[rows, lanes(c)] for c in range(8)],
            [vis_ref[c, rows, :].astype(F32) for c in range(8)],
            [gr[rows, lanes(c)] for c in range(8)],
        )
        for c in range(8):
            cal[rows, lanes(c)] = result[c].astype(BF16)
        return carry

    lax.fori_loop(0, nb // 16, step, 0)

    for u in range(UNITS[0]):
        for c in range(8):
            wide[pl.ds(u * 8 + c, 32, ROWS), :] = cal[u * 32 : (u + 1) * 32, lanes(c)].astype(F32)
    for level in (1, 2):
        packed = 1 << level
        width = 128 >> level
        src = iota((128 * packed, 128), 0)
        mean = jnp.where(
            iota((128 * packed, 128), 1) == (src >> 7) * width + ((src & 127) >> level), 1.0 / packed, 0.0
        ).astype(BF16)
        first = BASE[level] * 32
        for g in range(8 // packed):
            cols = slice(g * packed * 128, (g + 1) * packed * 128)
            value = dot(cal[first : first + UNITS[level] * 32, cols], mean)
            for u in range(UNITS[level]):
                row = ROW0[level] + u * (8 // packed) + g
                wide[pl.ds(row, 32, ROWS), :] = value[u * 32 : (u + 1) * 32]
    for m in range(32):
        out_ref[m, 0:ROWS, :] = wide[m * ROWS : (m + 1) * ROWS, :].astype(BF16)

    for level in (1, 2):
        group = iota((256, 256), 0) >> level == iota((256, 256), 1) >> level
        mean = jnp.where(group, 0.5**level, 0.0).astype(BF16)
        rows = slice(BASE[level] * 32, (BASE[level] + UNITS[level]) * 32)
        for c in range(0, 8, 2):
            cols = slice(c * 128, (c + 2) * 128)
            cal[rows, cols] = dot(cal[rows, cols], mean).astype(BF16)
    for c in range(0, 8, 2):
        part = dot(weight_ref[...], cal[:, c * 128 : (c + 2) * 128])
        for m in range(32):
            for half in range(2):
                row = ROWS + (c + half) * 8
                out_ref[m, row : row + 8, :] = part[m * 8 : (m + 1) * 8, lanes(half)].astype(BF16)


def calibrate(gains, left, right, weight, vis):
    nb = left.shape[0]
    vmem = pl.BlockSpec(memory_space=pltpu.VMEM)
    return pl.pallas_call(
        calibrate_kernel,
        in_specs=[vmem] * 5,
        out_specs=vmem,
        out_shape=jax.ShapeDtypeStruct((32, ROWS + 64, 128), BF16),
        scratch_shapes=[
            pltpu.VMEM((256, 1024), F32),
            pltpu.VMEM((nb, 1024), F32),
            pltpu.VMEM((nb, 1024), F32),
            pltpu.VMEM((nb, 1024), BF16),
            pltpu.VMEM((32 * ROWS, 128), F32),
        ],
        compiler_params=pltpu.CompilerParams(vmem_limit_bytes=VMEM_LIMIT),
        name="calibrate",
    )(gains, left, right, weight, vis)


def finish_kernel(recv_ref, pick_ref, lane_ref, time_ref, avg_ref, grid_ref, means):
    for r in range(0, ROWS, 8):
        level = time_ref[r : r + 8, :]
        at_least = [level >= 1.0, level >= 2.0, level >= 3.0]
        for x in range(0, 32, 8):
            value = [recv_ref[x + j, r : r + 8, :].astype(F32) for j in range(8)]
            two = [0.5 * (value[2 * j] + value[2 * j + 1]) for j in range(4)]
            four = [0.5 * (two[2 * j] + two[2 * j + 1]) for j in range(2)]
            eight = 0.5 * (four[0] + four[1])
            top = [jnp.where(at_least[2], eight, four[j]) for j in range(2)]
            mid = [jnp.where(at_least[1], top[j // 2], two[j]) for j in range(4)]
            for j in range(8):
                means[x + j, r : r + 8, :] = jnp.where(at_least[0], mid[j // 2], value[j])

    pick = pick_ref[:, 0:ROWS]
    lane = lane_ref[...]

    def step(i, carry):
        both = jnp.concatenate([means[2 * i], means[2 * i + 1]], axis=1).astype(BF16)
        rows = dot(pick, both)
        for half in range(2):
            value = jnp.take_along_axis(rows[:, lanes(half)], lane, axis=1, mode="promise_in_bounds")
            avg_ref[2 * i + half] = value.astype(BF16).reshape(8, 16, 128)
        return carry

    lax.fori_loop(0, 16, step, 0)

    for c in range(8):
        row = ROWS + c * 8
        total = recv_ref[0, row : row + 8, :].astype(F32)
        for t in range(1, 32):
            total = total + recv_ref[t, row : row + 8, :].astype(F32)
        for u in range(8):
            grid_ref[u, c : c + 1, :] = total[u : u + 1, :]


def finish(recv, pick, lane, time):
    vmem = pl.BlockSpec(memory_space=pltpu.VMEM)
    return pl.pallas_call(
        finish_kernel,
        in_specs=[vmem] * 4,
        out_specs=[vmem] * 2,
        out_shape=[
            jax.ShapeDtypeStruct((32, 8, 16, 128), BF16),
            jax.ShapeDtypeStruct((8, 8, 128), F32),
        ],
        scratch_shapes=[pltpu.VMEM((32, ROWS, 128), F32)],
        compiler_params=pltpu.CompilerParams(vmem_limit_bytes=VMEM_LIMIT),
        name="finish",
    )(recv, pick, lane, time)


def shards(visibilities, station_gains, station_pairs, average_bands, tile_map, baseline_order):
    me = lax.axis_index("tm").reshape(1)
    cut = cut_gains(station_gains)
    gains = lax.all_to_all(cut, "chan", 0, 0, tiled=True)
    moved, left, right, weight, pick, lane, time = prepare(
        me, station_pairs.T, average_bands.T, tile_map.T, baseline_order[None, :], visibilities[0]
    )
    payload = calibrate(gains, left, right, weight, moved)
    recv = lax.all_to_all(payload, "tm", 0, 0, tiled=True)
    averaged, gridded = finish(recv, pick, lane, time)
    return averaged, gridded


def solution(mesh):
    return jax.shard_map(
        shards,
        mesh=mesh,
        in_specs=(P("tm", None, None, "chan"), P(None, "chan", None), P(), P(), P(), P()),
        out_specs=(P(None, None, "tm", "chan"), P("tm", None, "chan")),
        check_vma=False,
    )
```

```python
import functools
import jax
import jax.numpy as jnp
from jax import lax
from jax.experimental import pallas as pl
from jax.experimental.pallas import tpu as pltpu
from jax.sharding import PartitionSpec as P

UNITS = (5, 5, 6)
BASE = (0, 5, 10)
ROW0 = (0, 40, 60)
ROWS = 72
F32 = jnp.float32
BF16 = jnp.bfloat16
VMEM_LIMIT = 24 << 20


def iota(shape, axis):
    return lax.broadcasted_iota(jnp.int32, shape, axis)


def one_hot(mask):
    return jnp.where(mask, 1.0, 0.0).astype(BF16)


def dot(a, b):
    return lax.dot_general(a, b, (((1,), (0,)), ((), ())), preferred_element_type=F32)


def dot_t(a, b):
    return lax.dot_general(a, b, (((1,), (1,)), ((), ())), preferred_element_type=F32)


def rows_of(values, width):
    row = iota((8, width), 0)
    result = jnp.zeros((8, width), F32)
    for i, value in enumerate(values):
        result = jnp.where(row == i, value, result)
    return result


def gains_kernel(gain_ref, out_ref):
    for d in range(8):
        out_ref[d] = gain_ref[:, :, d * 128 : (d + 1) * 128].astype(BF16)


def cut_gains(gains):
    comps, stations, _ = gains.shape
    return pl.pallas_call(
        gains_kernel,
        out_shape=jax.ShapeDtypeStruct((8, comps, stations, 128), BF16),
        compiler_params=pltpu.CompilerParams(vmem_limit_bytes=VMEM_LIMIT),
        name="cut_gains",
    )(gains)


def prepare_kernel(
    me_ref, pairs_ref, bands_ref, tiles_ref, order_ref, vis_ref,
    vis_out, left_out, right_out, weight_out, pick_out, lane_out, time_out,
):
    me = me_ref[0]
    nb = order_ref.shape[1]
    time_level = bands_ref[0:1, :]
    chan_level = bands_ref[1:2, :]
    tile = tiles_ref[pl.ds(me, 1), :]
    for level in range(1, 4):
        start = (me >> level) << level
        tile = jnp.where(time_level == level, tiles_ref[pl.ds(start, 1), :], tile)
    info = rows_of(
        [time_level.astype(F32), chan_level.astype(F32), tile.astype(F32)], nb
    ).astype(BF16)

    order_hot = one_hot(iota((nb, nb), 0) == order_ref[...])
    at_position = dot(info, order_hot)
    chan_here = at_position[1:2, :]
    same = rows_of([jnp.where(chan_here == float(level), 1.0, 0.0) for level in range(3)], nb)
    before = one_hot(
        (iota((nb, nb), 0) < iota((nb, nb), 1)) & ((iota((nb, nb), 0) >> 4) == (iota((nb, nb), 1) >> 4))
    )
    count = dot(same.astype(BF16), before)
    unit = jnp.where(
        chan_here == 0.0,
        count[0:1, :],
        jnp.where(chan_here == 1.0, BASE[1] + count[1:2, :], BASE[2] + count[2:3, :]),
    )
    block = iota((1, nb), 1) >> 4
    slot = unit.astype(jnp.int32) * 32 + block
    slot_hot = dot_t(one_hot(iota((nb, nb), 0) == slot), order_hot).astype(BF16)

    for c in range(0, 8, 2):
        both = jnp.concatenate([vis_ref[c], vis_ref[c + 1]], axis=1)
        moved = dot(slot_hot, both).astype(BF16)
        vis_out[c] = moved[:, :128]
        vis_out[c + 1] = moved[:, 128:]

    left_out[...] = dot_t(slot_hot, one_hot(iota((256, nb), 0) == pairs_ref[0:1, :])).astype(BF16)
    right_out[...] = dot_t(slot_hot, one_hot(iota((256, nb), 0) == pairs_ref[1:2, :])).astype(BF16)

    at_slot = dot_t(info, slot_hot)
    time_slot = at_slot[0:1, :]
    weight = jnp.where(
        time_slot == 0.0, 1.0, jnp.where(time_slot == 1.0, 0.5, jnp.where(time_slot == 2.0, 0.25, 0.125))
    )
    tile_slot = at_slot[2:3, :].astype(jnp.int32)
    weight_out[...] = jnp.where(iota((256, nb), 0) == tile_slot, weight, 0.0).astype(BF16)

    lane = iota((1, 128), 1)
    own = rows_of([at_position[0:1, :], chan_here, unit], nb).astype(BF16)
    own = dot(own, one_hot(iota((nb, 128), 0) == me * 16 + (iota((nb, 128), 1) & 15)))
    own_time = own[0:1, :]
    own_chan = own[1:2, :].astype(jnp.int32)
    own_unit = own[2:3, :].astype(jnp.int32)
    comp = lane >> 4
    packed_row = jnp.where(
        own_chan == 0,
        own_unit * 8 + comp,
        jnp.where(
            own_chan == 1,
            ROW0[1] + (own_unit - BASE[1]) * 4 + (comp >> 1),
            ROW0[2] + (own_unit - BASE[2]) * 2 + (comp >> 2),
        ),
    )
    part = jnp.where(own_chan == 0, 0, jnp.where(own_chan == 1, 1 + (comp & 1), 3 + (comp & 3)))
    sub = iota((128, 128), 0)
    lan = iota((128, 128), 1)
    eye = one_hot(sub == lan)
    row_hot = one_hot(sub == packed_row)
    pick_out[...] = dot_t(eye, row_hot).astype(BF16)
    part_hot = dot_t(eye, one_hot(sub == part)).astype(BF16)
    table = jnp.where(
        sub == 0,
        lan,
        jnp.where(sub <= 2, (sub - 1) * 64 + (lan >> 1), jnp.where(sub <= 6, (sub - 3) * 32 + (lan >> 2), 0)),
    )
    lane_out[...] = dot(part_hot, table.astype(F32).astype(BF16)).astype(jnp.int32)
    share = jnp.where(sub < ROW0[1], 1.0, jnp.where(sub < ROW0[2], 0.5, 0.25))
    spread = jnp.broadcast_to(own_time, (128, 128)).astype(BF16)
    time_out[...] = dot_t(row_hot, spread) * share


def prepare(me, pairs, bands, tiles, order, vis):
    nb = order.shape[1]
    vmem = pl.BlockSpec(memory_space=pltpu.VMEM)
    return pl.pallas_call(
        prepare_kernel,
        in_specs=[pl.BlockSpec(memory_space=pltpu.SMEM)] + [vmem] * 5,
        out_specs=[vmem] * 7,
        out_shape=[
            jax.ShapeDtypeStruct((8, nb, 128), BF16),
            jax.ShapeDtypeStruct((nb, 256), BF16),
            jax.ShapeDtypeStruct((nb, 256), BF16),
            jax.ShapeDtypeStruct((256, nb), BF16),
            jax.ShapeDtypeStruct((128, 128), BF16),
            jax.ShapeDtypeStruct((128, 128), jnp.int32),
            jax.ShapeDtypeStruct((128, 128), F32),
        ],
        compiler_params=pltpu.CompilerParams(vmem_limit_bytes=VMEM_LIMIT),
        cost_estimate=pl.CostEstimate(flops=2_000_000_000, bytes_accessed=4_000_000, transcendentals=0),
        name="prepare",
    )(me, pairs, bands, tiles, order, vis)


def product(left, right):
    return (left[0] * right[0] - left[1] * right[1], left[0] * right[1] + left[1] * right[0])


def product_conj(left, right):
    return (left[0] * right[0] + left[1] * right[1], left[1] * right[0] - left[0] * right[1])


def add_pair(left, right):
    return (left[0] + right[0], left[1] + right[1])


def as_matrix(components):
    return [
        [(components[0], components[1]), (components[2], components[3])],
        [(components[4], components[5]), (components[6], components[7])],
    ]


def jones_apply(first, middle, second):
    left_gain = as_matrix(first)
    coherency = as_matrix(middle)
    right_gain = as_matrix(second)
    partial_rows = [
        [
            add_pair(
                product(left_gain[i][0], coherency[0][k]), product(left_gain[i][1], coherency[1][k])
            )
            for k in range(2)
        ]
        for i in range(2)
    ]
    result = []
    for i in range(2):
        for c in range(2):
            element = add_pair(
                product_conj(partial_rows[i][0], right_gain[c][0]),
                product_conj(partial_rows[i][1], right_gain[c][1]),
            )
            result.extend(element)
    return result


def lanes(c):
    return slice(c * 128, (c + 1) * 128)


def calibrate_kernel(gain_ref, left_ref, right_ref, weight_ref, vis_ref, out_ref, gains, gl, gr, cal, wide):
    nb = left_ref.shape[0]
    stations = gain_ref.shape[2]
    for d in range(8):
        for c in range(8):
            gains[d * stations : (d + 1) * stations, lanes(c)] = gain_ref[d, c].astype(F32)
    gains[8 * stations :, :] = jnp.zeros((256 - 8 * stations, 1024), F32)
    table = gains[...].astype(BF16)
    gl[...] = dot(left_ref[...], table)
    gr[...] = dot(right_ref[...], table)

    def step(i, carry):
        rows = pl.ds(pl.multiple_of(i * 16, 16), 16)
        result = jones_apply(
            [gl[rows, lanes(c)] for c in range(8)],
            [vis_ref[c, rows, :].astype(F32) for c in range(8)],
            [gr[rows, lanes(c)] for c in range(8)],
        )
        for c in range(8):
            cal[rows, lanes(c)] = result[c].astype(BF16)
        return carry

    lax.fori_loop(0, nb // 16, step, 0, unroll=2)

    for u in range(UNITS[0]):
        for c in range(8):
            wide[pl.ds(u * 8 + c, 32, ROWS), :] = cal[u * 32 : (u + 1) * 32, lanes(c)].astype(F32)
    for level in (1, 2):
        packed = 1 << level
        width = 128 >> level
        src = iota((128 * packed, 128), 0)
        mean = jnp.where(
            iota((128 * packed, 128), 1) == (src >> 7) * width + ((src & 127) >> level), 1.0 / packed, 0.0
        ).astype(BF16)
        first = BASE[level] * 32
        for g in range(8 // packed):
            cols = slice(g * packed * 128, (g + 1) * packed * 128)
            value = dot(cal[first : first + UNITS[level] * 32, cols], mean)
            for u in range(UNITS[level]):
                row = ROW0[level] + u * (8 // packed) + g
                wide[pl.ds(row, 32, ROWS), :] = value[u * 32 : (u + 1) * 32]
    for m in range(32):
        out_ref[m, 0:ROWS, :] = wide[m * ROWS : (m + 1) * ROWS, :].astype(BF16)

    for level in (1, 2):
        group = iota((256, 256), 0) >> level == iota((256, 256), 1) >> level
        mean = jnp.where(group, 0.5**level, 0.0).astype(BF16)
        rows = slice(BASE[level] * 32, (BASE[level] + UNITS[level]) * 32)
        for c in range(0, 8, 2):
            cols = slice(c * 128, (c + 2) * 128)
            cal[rows, cols] = dot(cal[rows, cols], mean).astype(BF16)
    for c in range(0, 8, 2):
        part = dot(weight_ref[...], cal[:, c * 128 : (c + 2) * 128])
        for m in range(32):
            for half in range(2):
                row = ROWS + (c + half) * 8
                out_ref[m, row : row + 8, :] = part[m * 8 : (m + 1) * 8, lanes(half)].astype(BF16)


def calibrate(gains, left, right, weight, vis):
    nb = left.shape[0]
    vmem = pl.BlockSpec(memory_space=pltpu.VMEM)
    return pl.pallas_call(
        calibrate_kernel,
        in_specs=[vmem] * 5,
        out_specs=vmem,
        out_shape=jax.ShapeDtypeStruct((32, ROWS + 64, 128), BF16),
        scratch_shapes=[
            pltpu.VMEM((256, 1024), F32),
            pltpu.VMEM((nb, 1024), F32),
            pltpu.VMEM((nb, 1024), F32),
            pltpu.VMEM((nb, 1024), BF16),
            pltpu.VMEM((32 * ROWS, 128), F32),
        ],
        compiler_params=pltpu.CompilerParams(vmem_limit_bytes=VMEM_LIMIT),
        name="calibrate",
    )(gains, left, right, weight, vis)


def finish_kernel(recv_ref, pick_ref, lane_ref, time_ref, avg_ref, grid_ref, means):
    for r in range(0, ROWS, 8):
        level = time_ref[r : r + 8, :]
        at_least = [level >= 1.0, level >= 2.0, level >= 3.0]
        for x in range(0, 32, 8):
            value = [recv_ref[x + j, r : r + 8, :].astype(F32) for j in range(8)]
            two = [0.5 * (value[2 * j] + value[2 * j + 1]) for j in range(4)]
            four = [0.5 * (two[2 * j] + two[2 * j + 1]) for j in range(2)]
            eight = 0.5 * (four[0] + four[1])
            top = [jnp.where(at_least[2], eight, four[j]) for j in range(2)]
            mid = [jnp.where(at_least[1], top[j // 2], two[j]) for j in range(4)]
            for j in range(8):
                means[x + j, r : r + 8, :] = jnp.where(at_least[0], mid[j // 2], value[j])

    pick = pick_ref[:, 0:ROWS]
    lane = lane_ref[...]

    def step(i, carry):
        both = jnp.concatenate([means[2 * i], means[2 * i + 1]], axis=1).astype(BF16)
        rows = dot(pick, both)
        for half in range(2):
            value = jnp.take_along_axis(rows[:, lanes(half)], lane, axis=1, mode="promise_in_bounds")
            avg_ref[2 * i + half] = value.astype(BF16).reshape(8, 16, 128)
        return carry

    lax.fori_loop(0, 16, step, 0, unroll=8)

    for c in range(8):
        row = ROWS + c * 8
        total = recv_ref[0, row : row + 8, :].astype(F32)
        for t in range(1, 32):
            total = total + recv_ref[t, row : row + 8, :].astype(F32)
        for u in range(8):
            grid_ref[u, c : c + 1, :] = total[u : u + 1, :]


def finish(recv, pick, lane, time):
    vmem = pl.BlockSpec(memory_space=pltpu.VMEM)
    return pl.pallas_call(
        finish_kernel,
        in_specs=[vmem] * 4,
        out_specs=[vmem] * 2,
        out_shape=[
            jax.ShapeDtypeStruct((32, 8, 16, 128), BF16),
            jax.ShapeDtypeStruct((8, 8, 128), F32),
        ],
        scratch_shapes=[pltpu.VMEM((32, ROWS, 128), F32)],
        compiler_params=pltpu.CompilerParams(vmem_limit_bytes=VMEM_LIMIT),
        name="finish",
    )(recv, pick, lane, time)


def shards(visibilities, station_gains, station_pairs, average_bands, tile_map, baseline_order):
    me = lax.axis_index("tm").reshape(1)
    cut = cut_gains(station_gains)
    gains = lax.all_to_all(cut, "chan", 0, 0, tiled=True)
    moved, left, right, weight, pick, lane, time = prepare(
        me, station_pairs.T, average_bands.T, tile_map.T, baseline_order[None, :], visibilities[0]
    )
    payload = calibrate(gains, left, right, weight, moved)
    recv = lax.all_to_all(payload, "tm", 0, 0, tiled=True)
    averaged, gridded = finish(recv, pick, lane, time)
    return averaged, gridded


def solution(mesh):
    return jax.shard_map(
        shards,
        mesh=mesh,
        in_specs=(P("tm", None, None, "chan"), P(None, "chan", None), P(), P(), P(), P()),
        out_specs=(P(None, None, "tm", "chan"), P("tm", None, "chan")),
        check_vma=False,
    )
```

```python
import functools
import jax
import jax.numpy as jnp
from jax import lax
from jax.experimental import pallas as pl
from jax.experimental.pallas import tpu as pltpu
from jax.sharding import PartitionSpec as P

KEEP = 320
SEND = 192
FIRST = (0, 96, 192)
SIZES = (96, 96, 128)
UNIT_ROW = (0, 16, 24, 8, 32, 36, 12, 14, 40, 42)
ROWS = 48
MEANS = 80
F32 = jnp.float32
BF16 = jnp.bfloat16
VMEM_LIMIT = 24 << 20


def iota(shape, axis):
    return lax.broadcasted_iota(jnp.int32, shape, axis)


def one_hot(mask):
    return jnp.where(mask, 1.0, 0.0).astype(BF16)


def dot(a, b):
    return lax.dot_general(a, b, (((1,), (0,)), ((), ())), preferred_element_type=F32)


def dot_t(a, b):
    return lax.dot_general(a, b, (((1,), (1,)), ((), ())), preferred_element_type=F32)


def rows_of(values, width):
    row = iota((8, width), 0)
    result = jnp.zeros((8, width), F32)
    for i, value in enumerate(values):
        result = jnp.where(row == i, value, result)
    return result


def gains_kernel(gain_ref, after_ref, out_ref):
    del after_ref
    for d in range(8):
        out_ref[d] = gain_ref[:, :, d * 128 : (d + 1) * 128].astype(BF16)


def cut_gains(gains, after):
    comps, stations, _ = gains.shape
    return pl.pallas_call(
        gains_kernel,
        in_specs=[pl.BlockSpec(memory_space=pltpu.VMEM), pl.BlockSpec(memory_space=pl.ANY)],
        out_shape=jax.ShapeDtypeStruct((8, comps, stations, 128), BF16),
        compiler_params=pltpu.CompilerParams(vmem_limit_bytes=VMEM_LIMIT),
        name="cut_gains",
    )(gains, after)


def route_kernel(me_ref, bands_ref, order_ref, vis_ref, keep_out, send_out, hot_out, position_out):
    me = me_ref[0]
    nb = order_ref.shape[1]
    info = rows_of([bands_ref[0:1, :].astype(F32), bands_ref[1:2, :].astype(F32)], nb).astype(BF16)
    order_hot = one_hot(iota((nb, nb), 0) == order_ref[...])
    at_position = dot(info, order_hot)
    time_here = at_position[0:1, :]
    chan_here = at_position[1:2, :].astype(jnp.int32)
    kind = jnp.where(time_here == 0.0, 0, 3) + chan_here
    same = rows_of([jnp.where(kind == i, 1.0, 0.0) for i in range(6)], nb)
    before = one_hot(
        (iota((nb, nb), 0) < iota((nb, nb), 1)) & ((iota((nb, nb), 0) >> 4) == (iota((nb, nb), 1) >> 4))
    )
    counts = dot(same.astype(BF16), before)
    count = counts[0:1, :]
    for i in range(1, 6):
        count = jnp.where(kind == i, counts[i : i + 1, :], count)
    count = count.astype(jnp.int32)
    side = jnp.where(kind < 3, 0, count >> 1)
    place = jnp.where(kind < 3, count, count & 1)
    kept = jnp.where(chan_here == 0, 1, jnp.where(chan_here == 1, 4, 8)) + place
    sent = 10 + 2 * chan_here + place
    single = jnp.where(chan_here == 0, 0, jnp.where(chan_here == 1, 3, 6)) + place
    unit = jnp.where(kind < 3, single, jnp.where(side == (me & 1), kept, sent))
    slot = unit * 32 + (iota((1, nb), 1) >> 4)
    slot_hot = dot_t(one_hot(iota((nb, nb), 0) == slot), order_hot).astype(BF16)
    for c in range(0, 8, 2):
        both = jnp.concatenate([vis_ref[c], vis_ref[c + 1]], axis=1)
        moved = dot(slot_hot, both).astype(BF16)
        for half in range(2):
            keep_out[c + half] = moved[:KEEP, lanes(half)]
            send_out[c + half] = moved[KEEP:, lanes(half)]
    hot_out[...] = slot_hot[:KEEP]
    position_out[...] = rows_of(
        [time_here, chan_here.astype(F32), kind.astype(F32), side.astype(F32), place.astype(F32)], nb
    )


def route(me, bands, order, vis):
    nb = order.shape[1]
    vmem = pl.BlockSpec(memory_space=pltpu.VMEM)
    return pl.pallas_call(
        route_kernel,
        in_specs=[pl.BlockSpec(memory_space=pltpu.SMEM)] + [vmem] * 3,
        out_shape=[
            jax.ShapeDtypeStruct((8, KEEP, 128), BF16),
            jax.ShapeDtypeStruct((8, SEND, 128), BF16),
            jax.ShapeDtypeStruct((KEEP, nb), BF16),
            jax.ShapeDtypeStruct((8, nb), F32),
        ],
        compiler_params=pltpu.CompilerParams(vmem_limit_bytes=VMEM_LIMIT),
        name="route",
    )(me, bands, order, vis)


def tables_kernel(
    me_ref, pairs_ref, bands_ref, tiles_ref, hot_ref, position_ref,
    left_out, right_out, weight_out, pick_out, lane_out, time_out,
):
    me = me_ref[0]
    nb = pairs_ref.shape[1]
    time_level = bands_ref[0:1, :]
    tile = tiles_ref[pl.ds(me, 1), :]
    for level in range(1, 4):
        start = (me >> level) << level
        tile = jnp.where(time_level == level, tiles_ref[pl.ds(start, 1), :], tile)
    info = rows_of([time_level.astype(F32), tile.astype(F32)], nb).astype(BF16)
    slot_hot = hot_ref[...]
    left_out[...] = dot_t(slot_hot, one_hot(iota((256, nb), 0) == pairs_ref[0:1, :])).astype(BF16)
    right_out[...] = dot_t(slot_hot, one_hot(iota((256, nb), 0) == pairs_ref[1:2, :])).astype(BF16)

    at_slot = dot_t(info, slot_hot)
    time_slot = at_slot[0:1, :]
    weight = jnp.where(time_slot <= 1.0, 1.0, jnp.where(time_slot == 2.0, 0.5, 0.25))
    tile_slot = at_slot[1:2, :].astype(jnp.int32)
    weight_out[...] = jnp.where(iota((256, KEEP), 0) == tile_slot, weight, 0.0).astype(BF16)

    own = dot(
        position_ref[...].astype(BF16), one_hot(iota((nb, 128), 0) == me * 16 + (iota((nb, 128), 1) & 15))
    )
    own_time = own[0:1, :]
    own_chan = own[1:2, :].astype(jnp.int32)
    own_kind = own[2:3, :].astype(jnp.int32)
    own_side = own[3:4, :].astype(jnp.int32)
    own_place = own[4:5, :].astype(jnp.int32)
    comp = iota((1, 128), 1) >> 4
    within = jnp.where(
        own_chan == 0,
        own_place * 8 + comp,
        jnp.where(own_chan == 1, own_place * 4 + (comp >> 1), own_place * 2 + (comp >> 2)),
    )
    single = jnp.where(own_chan == 0, 0, jnp.where(own_chan == 1, 8, 12))
    sided = 16 + 32 * own_side + jnp.where(own_chan == 0, 0, jnp.where(own_chan == 1, 16, 24))
    packed_row = jnp.where(own_kind < 3, single, sided) + within
    part = jnp.where(own_chan == 0, 0, jnp.where(own_chan == 1, 1 + (comp & 1), 3 + (comp & 3)))
    sub = iota((128, 128), 0)
    lan = iota((128, 128), 1)
    eye = one_hot(sub == lan)
    row_hot = one_hot(sub == packed_row)
    pick_out[...] = dot_t(eye, row_hot).astype(BF16)
    part_hot = dot_t(eye, one_hot(sub == part)).astype(BF16)
    table = jnp.where(
        sub == 0,
        lan,
        jnp.where(sub <= 2, (sub - 1) * 64 + (lan >> 1), jnp.where(sub <= 6, (sub - 3) * 32 + (lan >> 2), 0)),
    )
    lane_out[...] = dot(part_hot, table.astype(F32).astype(BF16)).astype(jnp.int32)
    inner = (sub - 16) & 31
    level_of = jnp.where(sub < 8, 0, jnp.where(sub < 12, 1, 2))
    level_of = jnp.where(sub < 16, level_of, jnp.where(inner < 16, 0, jnp.where(inner < 24, 1, 2)))
    share = jnp.where(level_of == 0, 1.0, jnp.where(level_of == 1, 0.5, 0.25))
    spread = jnp.broadcast_to(own_time, (128, 128)).astype(BF16)
    time_out[...] = dot_t(row_hot, spread) * share


def tables(me, pairs, bands, tiles, hot, position):
    vmem = pl.BlockSpec(memory_space=pltpu.VMEM)
    nb = pairs.shape[1]
    return pl.pallas_call(
        tables_kernel,
        in_specs=[pl.BlockSpec(memory_space=pltpu.SMEM)] + [vmem] * 5,
        out_shape=[
            jax.ShapeDtypeStruct((KEEP, 256), BF16),
            jax.ShapeDtypeStruct((KEEP, 256), BF16),
            jax.ShapeDtypeStruct((256, KEEP), BF16),
            jax.ShapeDtypeStruct((128, 128), BF16),
            jax.ShapeDtypeStruct((128, 128), jnp.int32),
            jax.ShapeDtypeStruct((128, 128), F32),
        ],
        compiler_params=pltpu.CompilerParams(vmem_limit_bytes=VMEM_LIMIT),
        cost_estimate=pl.CostEstimate(flops=1_000_000_000, bytes_accessed=4_000_000, transcendentals=0),
        name="tables",
    )(me, pairs, bands, tiles, hot, position)


def product(left, right):
    return (left[0] * right[0] - left[1] * right[1], left[0] * right[1] + left[1] * right[0])


def product_conj(left, right):
    return (left[0] * right[0] + left[1] * right[1], left[1] * right[0] - left[0] * right[1])


def add_pair(left, right):
    return (left[0] + right[0], left[1] + right[1])


def as_matrix(components):
    return [
        [(components[0], components[1]), (components[2], components[3])],
        [(components[4], components[5]), (components[6], components[7])],
    ]


def jones_apply(first, middle, second):
    left_gain = as_matrix(first)
    coherency = as_matrix(middle)
    right_gain = as_matrix(second)
    partial_rows = [
        [
            add_pair(
                product(left_gain[i][0], coherency[0][k]), product(left_gain[i][1], coherency[1][k])
            )
            for k in range(2)
        ]
        for i in range(2)
    ]
    result = []
    for i in range(2):
        for c in range(2):
            element = add_pair(
                product_conj(partial_rows[i][0], right_gain[c][0]),
                product_conj(partial_rows[i][1], right_gain[c][1]),
            )
            result.extend(element)
    return result


def lanes(c):
    return slice(c * 128, (c + 1) * 128)


def calibrate_kernel(gain_ref, left_ref, right_ref, weight_ref, vis_ref, pair_ref, out_ref, gains, gl, gr, cal, wide):
    stations = gain_ref.shape[2]
    for d in range(8):
        for c in range(8):
            gains[d * stations : (d + 1) * stations, lanes(c)] = gain_ref[d, c].astype(F32)
    gains[8 * stations :, :] = jnp.zeros((256 - 8 * stations, 1024), F32)
    table = gains[...].astype(BF16)
    gl[...] = dot(left_ref[...], table)
    gr[...] = dot(right_ref[...], table)

    def block(first, value):
        rows = pl.ds(pl.multiple_of(first, 16), 16)
        result = jones_apply(
            [gl[rows, lanes(c)] for c in range(8)],
            [value(c, rows) for c in range(8)],
            [gr[rows, lanes(c)] for c in range(8)],
        )
        for c in range(8):
            cal[rows, lanes(c)] = result[c].astype(BF16)

    for level, singles in ((0, 32), (1, 32), (2, 64)):

        def single(i, carry, level=level):
            block(FIRST[level] + i * 16, lambda c, rows: vis_ref[c, rows, :].astype(F32))
            return carry

        def paired(i, carry, level=level, singles=singles):
            other = pl.ds(pl.multiple_of(level * 64 + i * 16, 16), 16)
            block(
                FIRST[level] + singles + i * 16,
                lambda c, rows: 0.5 * (vis_ref[c, rows, :].astype(F32) + pair_ref[c, other, :].astype(F32)),
            )
            return carry

        lax.fori_loop(0, singles // 16, single, 0, unroll=2)
        lax.fori_loop(0, 4, paired, 0, unroll=2)

    for u in range(3):
        for c in range(8):
            wide[pl.ds(UNIT_ROW[u] + c, 32, ROWS), :] = cal[u * 32 : (u + 1) * 32, lanes(c)].astype(F32)
    for level in (1, 2):
        packed = 1 << level
        width = 128 >> level
        src = iota((128 * packed, 128), 0)
        mean = jnp.where(
            iota((128 * packed, 128), 1) == (src >> 7) * width + ((src & 127) >> level), 1.0 / packed, 0.0
        ).astype(BF16)
        first = FIRST[level]
        for g in range(8 // packed):
            cols = slice(g * packed * 128, (g + 1) * packed * 128)
            value = dot(cal[first : first + SIZES[level], cols], mean)
            for u in range(SIZES[level] // 32):
                row = UNIT_ROW[first // 32 + u] + g
                wide[pl.ds(row, 32, ROWS), :] = value[u * 32 : (u + 1) * 32]
    for row in range(44, ROWS):
        wide[pl.ds(row, 32, ROWS), :] = jnp.zeros((32, 128), F32)
    for m in range(32):
        out_ref[m, 0:ROWS, :] = wide[m * ROWS : (m + 1) * ROWS, :].astype(BF16)

    for level in (1, 2):
        group = iota((256, 256), 0) >> level == iota((256, 256), 1) >> level
        mean = jnp.where(group, 0.5**level, 0.0).astype(BF16)
        rows = slice(FIRST[level], FIRST[level] + SIZES[level])
        for c in range(0, 8, 2):
            cols = slice(c * 128, (c + 2) * 128)
            cal[rows, cols] = dot(cal[rows, cols], mean).astype(BF16)
    for c in range(0, 8, 2):
        part = dot(weight_ref[...], cal[:, c * 128 : (c + 2) * 128])
        for m in range(32):
            for half in range(2):
                row = ROWS + (c + half) * 8
                out_ref[m, row : row + 8, :] = part[m * 8 : (m + 1) * 8, lanes(half)].astype(BF16)


def calibrate(gains, left, right, weight, vis, pair):
    vmem = pl.BlockSpec(memory_space=pltpu.VMEM)
    return pl.pallas_call(
        calibrate_kernel,
        in_specs=[vmem] * 6,
        out_specs=vmem,
        out_shape=jax.ShapeDtypeStruct((32, ROWS + 64, 128), BF16),
        scratch_shapes=[
            pltpu.VMEM((256, 1024), F32),
            pltpu.VMEM((KEEP, 1024), F32),
            pltpu.VMEM((KEEP, 1024), F32),
            pltpu.VMEM((KEEP, 1024), BF16),
            pltpu.VMEM((32 * ROWS, 128), F32),
        ],
        compiler_params=pltpu.CompilerParams(vmem_limit_bytes=VMEM_LIMIT),
        name="calibrate",
    )(gains, left, right, weight, vis, pair)


def finish_kernel(recv_ref, pick_ref, lane_ref, time_ref, avg_ref, grid_ref, means):
    for t in range(32):
        means[t, 0:16, :] = recv_ref[t, 0:16, :].astype(F32)
    for side in range(2):
        for r in range(16, ROWS, 8):
            row = r + 32 * side
            level = time_ref[row : row + 8, :]
            at_least = [level >= 2.0, level >= 3.0]
            for x in range(0, 32, 8):
                two = [recv_ref[x + 2 * j + side, r : r + 8, :].astype(F32) for j in range(4)]
                four = [0.5 * (two[2 * j] + two[2 * j + 1]) for j in range(2)]
                eight = 0.5 * (four[0] + four[1])
                top = [jnp.where(at_least[1], eight, four[j]) for j in range(2)]
                for j in range(4):
                    value = jnp.where(at_least[0], top[j // 2], two[j])
                    means[x + 2 * j, row : row + 8, :] = value
                    means[x + 2 * j + 1, row : row + 8, :] = value

    pick = pick_ref[:, 0:MEANS]
    lane = lane_ref[...]

    def step(i, carry):
        both = jnp.concatenate([means[2 * i], means[2 * i + 1]], axis=1).astype(BF16)
        rows = dot(pick, both)
        for half in range(2):
            value = jnp.take_along_axis(rows[:, lanes(half)], lane, axis=1, mode="promise_in_bounds")
            avg_ref[2 * i + half] = value.astype(BF16).reshape(8, 16, 128)
        return carry

    lax.fori_loop(0, 16, step, 0, unroll=8)

    for c in range(8):
        row = ROWS + c * 8
        total = recv_ref[0, row : row + 8, :].astype(F32)
        for t in range(1, 32):
            total = total + recv_ref[t, row : row + 8, :].astype(F32)
        for u in range(8):
            grid_ref[u, c : c + 1, :] = total[u : u + 1, :]


def finish(recv, pick, lane, time):
    vmem = pl.BlockSpec(memory_space=pltpu.VMEM)
    return pl.pallas_call(
        finish_kernel,
        in_specs=[vmem] * 4,
        out_specs=[vmem] * 2,
        out_shape=[
            jax.ShapeDtypeStruct((32, 8, 16, 128), BF16),
            jax.ShapeDtypeStruct((8, 8, 128), F32),
        ],
        scratch_shapes=[pltpu.VMEM((32, MEANS, 128), F32)],
        compiler_params=pltpu.CompilerParams(vmem_limit_bytes=VMEM_LIMIT),
        name="finish",
    )(recv, pick, lane, time)


def shards(visibilities, station_gains, station_pairs, average_bands, tile_map, baseline_order):
    me = lax.axis_index("tm").reshape(1)
    bands = average_bands.T
    keep, send, hot, position = route(me, bands, baseline_order[None, :], visibilities[0])
    pair = lax.ppermute(send, "tm", [(m, m ^ 1) for m in range(32)])
    gains = lax.all_to_all(cut_gains(station_gains, position), "chan", 0, 0, tiled=True)
    left, right, weight, pick, lane, time = tables(me, station_pairs.T, bands, tile_map.T, hot, position)
    payload = calibrate(gains, left, right, weight, keep, pair)
    recv = lax.all_to_all(payload, "tm", 0, 0, tiled=True)
    averaged, gridded = finish(recv, pick, lane, time)
    return averaged, gridded


def solution(mesh):
    return jax.shard_map(
        shards,
        mesh=mesh,
        in_specs=(P("tm", None, None, "chan"), P(None, "chan", None), P(), P(), P(), P()),
        out_specs=(P(None, None, "tm", "chan"), P("tm", None, "chan")),
        check_vma=False,
    )
```

```python
import functools
import jax
import jax.numpy as jnp
from jax import lax
from jax.experimental import pallas as pl
from jax.experimental.pallas import tpu as pltpu
from jax.sharding import PartitionSpec as P

KEEP = 320
SEND = 192
FIRST = (0, 96, 192)
SIZES = (96, 96, 128)
UNIT_ROW = (0, 16, 24, 8, 32, 36, 12, 14, 40, 42)
ROWS = 48
MEANS = 80
F32 = jnp.float32
BF16 = jnp.bfloat16
VMEM_LIMIT = 24 << 20


def iota(shape, axis):
    return lax.broadcasted_iota(jnp.int32, shape, axis)


def one_hot(mask):
    return jnp.where(mask, 1.0, 0.0).astype(BF16)


def dot(a, b):
    return lax.dot_general(a, b, (((1,), (0,)), ((), ())), preferred_element_type=F32)


def dot_t(a, b):
    return lax.dot_general(a, b, (((1,), (1,)), ((), ())), preferred_element_type=F32)


def roll64(value):
    return pltpu.roll(value, 64, 1)


def low_lanes(rows):
    return iota((rows, 128), 1) < 64


def rows_of(values, width):
    row = iota((8, width), 0)
    result = jnp.zeros((8, width), F32)
    for i, value in enumerate(values):
        result = jnp.where(row == i, value, result)
    return result


def gains_kernel(me_ref, gain_ref, after_ref, out_ref):
    del after_ref
    first_half = ((me_ref[0] >> 3) & 1) == 0
    stations = gain_ref.shape[1]
    low = low_lanes(stations)
    for d in range(8):
        for g in range(4):
            a = gain_ref[2 * g, :, d * 128 : (d + 1) * 128]
            b = gain_ref[2 * g + 1, :, d * 128 : (d + 1) * 128]
            a = jnp.where(first_half, a, roll64(a))
            b = jnp.where(first_half, roll64(b), b)
            out_ref[d, g * stations : (g + 1) * stations, :] = jnp.where(low, a, b).astype(BF16)


def cut_gains(me, gains, after):
    comps, stations, _ = gains.shape
    return pl.pallas_call(
        gains_kernel,
        in_specs=[
            pl.BlockSpec(memory_space=pltpu.SMEM),
            pl.BlockSpec(memory_space=pltpu.VMEM),
            pl.BlockSpec(memory_space=pl.ANY),
        ],
        out_shape=jax.ShapeDtypeStruct((8, comps // 2 * stations, 128), BF16),
        compiler_params=pltpu.CompilerParams(vmem_limit_bytes=VMEM_LIMIT),
        name="cut_gains",
    )(me, gains, after)


def route_kernel(me_ref, bands_ref, order_ref, vis_ref, keep_out, x_out, z_out, xz_out, hot_out, position_out):
    me = me_ref[0]
    nb = order_ref.shape[1]
    info = rows_of([bands_ref[0:1, :].astype(F32), bands_ref[1:2, :].astype(F32)], nb).astype(BF16)
    order_hot = one_hot(iota((nb, nb), 0) == order_ref[...])
    at_position = dot(info, order_hot)
    time_here = at_position[0:1, :]
    chan_here = at_position[1:2, :].astype(jnp.int32)
    kind = jnp.where(time_here == 0.0, 0, 3) + chan_here
    same = rows_of([jnp.where(kind == i, 1.0, 0.0) for i in range(6)], nb)
    before = one_hot(
        (iota((nb, nb), 0) < iota((nb, nb), 1)) & ((iota((nb, nb), 0) >> 4) == (iota((nb, nb), 1) >> 4))
    )
    counts = dot(same.astype(BF16), before)
    count = counts[0:1, :]
    for i in range(1, 6):
        count = jnp.where(kind == i, counts[i : i + 1, :], count)
    count = count.astype(jnp.int32)
    side = jnp.where(kind < 3, 0, count >> 1)
    place = jnp.where(kind < 3, count, count & 1)
    kept = jnp.where(chan_here == 0, 1, jnp.where(chan_here == 1, 4, 8)) + place
    sent = 10 + 2 * chan_here + place
    single = jnp.where(chan_here == 0, 0, jnp.where(chan_here == 1, 3, 6)) + place
    unit = jnp.where(kind < 3, single, jnp.where(side == (me & 1), kept, sent))
    slot = unit * 32 + (iota((1, nb), 1) >> 4)
    slot_hot = dot_t(one_hot(iota((nb, nb), 0) == slot), order_hot).astype(BF16)
    first_half = ((me >> 3) & 1) == 0
    low = low_lanes(nb)
    for g in range(4):
        both = jnp.concatenate([vis_ref[2 * g], vis_ref[2 * g + 1]], axis=1)
        moved = dot(slot_hot, both)
        a = moved[:, lanes(0)]
        b = moved[:, lanes(1)]
        keep_out[2 * g] = a[:KEEP].astype(BF16)
        keep_out[2 * g + 1] = b[:KEEP].astype(BF16)
        lower = jnp.where(low, a, roll64(b))
        upper = jnp.where(low, roll64(a), b)
        here = jnp.where(first_half, lower, upper).astype(BF16)
        there = jnp.where(first_half, upper, lower).astype(BF16)
        x_out[g] = there[:KEEP]
        xz_out[g] = there[KEEP:]
        z_out[g] = here[KEEP:]
    hot_out[...] = slot_hot[:KEEP]
    position_out[...] = rows_of(
        [time_here, chan_here.astype(F32), kind.astype(F32), side.astype(F32), place.astype(F32)], nb
    )


def route(me, bands, order, vis):
    nb = order.shape[1]
    vmem = pl.BlockSpec(memory_space=pltpu.VMEM)
    return pl.pallas_call(
        route_kernel,
        in_specs=[pl.BlockSpec(memory_space=pltpu.SMEM)] + [vmem] * 3,
        out_shape=[
            jax.ShapeDtypeStruct((8, KEEP, 128), BF16),
            jax.ShapeDtypeStruct((4, KEEP, 128), BF16),
            jax.ShapeDtypeStruct((4, SEND, 128), BF16),
            jax.ShapeDtypeStruct((4, SEND, 128), BF16),
            jax.ShapeDtypeStruct((KEEP, nb), BF16),
            jax.ShapeDtypeStruct((8, nb), F32),
        ],
        compiler_params=pltpu.CompilerParams(vmem_limit_bytes=VMEM_LIMIT),
        name="route",
    )(me, bands, order, vis)


def tables_kernel(
    me_ref, pairs_ref, bands_ref, tiles_ref, hot_ref, position_ref,
    left_out, right_out, weight_out, pick_out, lane_out, time_out,
):
    me = me_ref[0]
    nb = pairs_ref.shape[1]
    time_level = bands_ref[0:1, :]
    tiles = []
    for now in (me & ~8, me | 8):
        tile = tiles_ref[pl.ds(now, 1), :]
        for level in range(1, 4):
            start = (now >> level) << level
            tile = jnp.where(time_level == level, tiles_ref[pl.ds(start, 1), :], tile)
        tiles.append(tile.astype(F32))
    info = rows_of([time_level.astype(F32)] + tiles, nb).astype(BF16)
    slot_hot = hot_ref[...]
    left_out[...] = dot_t(slot_hot, one_hot(iota((256, nb), 0) == pairs_ref[0:1, :])).astype(BF16)
    right_out[...] = dot_t(slot_hot, one_hot(iota((256, nb), 0) == pairs_ref[1:2, :])).astype(BF16)

    at_slot = dot_t(info, slot_hot)
    time_slot = at_slot[0:1, :]
    weight = jnp.where(time_slot <= 1.0, 1.0, jnp.where(time_slot == 2.0, 0.5, 0.25))
    for i in range(2):
        tile_slot = at_slot[1 + i : 2 + i, :].astype(jnp.int32)
        weight_out[i] = jnp.where(iota((256, KEEP), 0) == tile_slot, weight, 0.0).astype(BF16)

    own = dot(
        position_ref[...].astype(BF16), one_hot(iota((nb, 128), 0) == me * 16 + (iota((nb, 128), 1) & 15))
    )
    own_time = own[0:1, :]
    own_chan = own[1:2, :].astype(jnp.int32)
    own_kind = own[2:3, :].astype(jnp.int32)
    own_side = own[3:4, :].astype(jnp.int32)
    own_place = own[4:5, :].astype(jnp.int32)
    comp = iota((1, 128), 1) >> 4
    within = jnp.where(
        own_chan == 0,
        own_place * 8 + comp,
        jnp.where(own_chan == 1, own_place * 4 + (comp >> 1), own_place * 2 + (comp >> 2)),
    )
    single = jnp.where(own_chan == 0, 0, jnp.where(own_chan == 1, 8, 12))
    sided = 16 + 32 * own_side + jnp.where(own_chan == 0, 0, jnp.where(own_chan == 1, 16, 24))
    packed_row = jnp.where(own_kind < 3, single, sided) + within
    part = jnp.where(own_chan == 0, 0, jnp.where(own_chan == 1, 1 + (comp & 1), 3 + (comp & 3)))
    sub = iota((128, 128), 0)
    lan = iota((128, 128), 1)
    eye = one_hot(sub == lan)
    row_hot = one_hot(sub == packed_row)
    pick_out[...] = dot_t(eye, row_hot).astype(BF16)
    part_hot = dot_t(eye, one_hot(sub == part)).astype(BF16)
    inside = lan & 63
    for bit in range(2):
        table = jnp.where(
            sub == 0,
            bit * 64 + inside,
            jnp.where(
                sub <= 2,
                (sub - 1) * 64 + bit * 32 + (inside >> 1),
                jnp.where(sub <= 6, (sub - 3) * 32 + bit * 16 + (inside >> 2), 0),
            ),
        )
        lane_out[bit] = dot(part_hot, table.astype(F32).astype(BF16)).astype(jnp.int32)
    inner = (sub - 16) & 31
    level_of = jnp.where(sub < 8, 0, jnp.where(sub < 12, 1, 2))
    level_of = jnp.where(sub < 16, level_of, jnp.where(inner < 16, 0, jnp.where(inner < 24, 1, 2)))
    share = jnp.where(level_of == 0, 1.0, jnp.where(level_of == 1, 0.5, 0.25))
    spread = jnp.broadcast_to(own_time, (128, 128)).astype(BF16)
    time_out[...] = dot_t(row_hot, spread) * share


def tables(me, pairs, bands, tiles, hot, position):
    vmem = pl.BlockSpec(memory_space=pltpu.VMEM)
    nb = pairs.shape[1]
    return pl.pallas_call(
        tables_kernel,
        in_specs=[pl.BlockSpec(memory_space=pltpu.SMEM)] + [vmem] * 5,
        out_shape=[
            jax.ShapeDtypeStruct((KEEP, 256), BF16),
            jax.ShapeDtypeStruct((KEEP, 256), BF16),
            jax.ShapeDtypeStruct((2, 256, KEEP), BF16),
            jax.ShapeDtypeStruct((128, 128), BF16),
            jax.ShapeDtypeStruct((2, 128, 128), jnp.int32),
            jax.ShapeDtypeStruct((128, 128), F32),
        ],
        compiler_params=pltpu.CompilerParams(vmem_limit_bytes=VMEM_LIMIT),
        cost_estimate=pl.CostEstimate(flops=1_000_000_000, bytes_accessed=4_000_000, transcendentals=0),
        name="tables",
    )(me, pairs, bands, tiles, hot, position)


def product(left, right):
    return (left[0] * right[0] - left[1] * right[1], left[0] * right[1] + left[1] * right[0])


def product_conj(left, right):
    return (left[0] * right[0] + left[1] * right[1], left[1] * right[0] - left[0] * right[1])


def add_pair(left, right):
    return (left[0] + right[0], left[1] + right[1])


def as_matrix(components):
    return [
        [(components[0], components[1]), (components[2], components[3])],
        [(components[4], components[5]), (components[6], components[7])],
    ]


def jones_apply(first, middle, second):
    left_gain = as_matrix(first)
    coherency = as_matrix(middle)
    right_gain = as_matrix(second)
    partial_rows = [
        [
            add_pair(
                product(left_gain[i][0], coherency[0][k]), product(left_gain[i][1], coherency[1][k])
            )
            for k in range(2)
        ]
        for i in range(2)
    ]
    result = []
    for i in range(2):
        for c in range(2):
            element = add_pair(
                product_conj(partial_rows[i][0], right_gain[c][0]),
                product_conj(partial_rows[i][1], right_gain[c][1]),
            )
            result.extend(element)
    return result


def lanes(c):
    return slice(c * 128, (c + 1) * 128)


def calibrate_kernel(
    me_ref, gain_ref, left_ref, right_ref, weight_ref, vis_ref, x_ref, z_ref, xz_ref, out_ref, gains, gl, gr, cal, wide
):
    stations = gain_ref.shape[1] // 4
    low = low_lanes(stations)
    for d in range(8):
        for g in range(4):
            both = gain_ref[d, g * stations : (g + 1) * stations, :].astype(F32)
            swapped = roll64(both)
            gains[d * stations : (d + 1) * stations, lanes(2 * g)] = jnp.where(low, both, swapped)
            gains[d * stations : (d + 1) * stations, lanes(2 * g + 1)] = jnp.where(low, swapped, both)
    gains[8 * stations :, :] = jnp.zeros((256 - 8 * stations, 1024), F32)
    table = gains[...].astype(BF16)
    gl[...] = dot(left_ref[...], table)
    gr[...] = dot(right_ref[...], table)

    first_half = ((me_ref[0] >> 3) & 1) == 0
    mine = low_lanes(16) == first_half

    def spread(ref, g, rows, front):
        both = ref[g, rows, :].astype(F32)
        swapped = roll64(both)
        return jnp.where(front, both, swapped), jnp.where(front, swapped, both)

    def block(first, other):
        rows = pl.ds(pl.multiple_of(first, 16), 16)
        value = []
        for g in range(4):
            theirs = spread(x_ref, g, rows, jnp.logical_not(first_half))
            pair = [jnp.where(mine, vis_ref[2 * g + i, rows, :].astype(F32), theirs[i]) for i in range(2)]
            if other is not None:
                near = spread(z_ref, g, other, first_half)
                far = spread(xz_ref, g, other, jnp.logical_not(first_half))
                pair = [0.5 * (pair[i] + jnp.where(mine, near[i], far[i])) for i in range(2)]
            value.extend(pair)
        result = jones_apply(
            [gl[rows, lanes(c)] for c in range(8)], value, [gr[rows, lanes(c)] for c in range(8)]
        )
        for c in range(8):
            cal[rows, lanes(c)] = result[c].astype(BF16)

    for level, singles in ((0, 32), (1, 32), (2, 64)):

        def single(i, carry, level=level):
            block(FIRST[level] + i * 16, None)
            return carry

        def paired(i, carry, level=level, singles=singles):
            other = pl.ds(pl.multiple_of(level * 64 + i * 16, 16), 16)
            block(FIRST[level] + singles + i * 16, other)
            return carry

        lax.fori_loop(0, singles // 16, single, 0, unroll=2)
        lax.fori_loop(0, 4, paired, 0, unroll=2)

    for u in range(3):
        for c in range(8):
            wide[pl.ds(UNIT_ROW[u] + c, 32, ROWS), :] = cal[u * 32 : (u + 1) * 32, lanes(c)].astype(F32)
    for level in (1, 2):
        packed = 1 << level
        width = 128 >> level
        src = iota((128 * packed, 128), 0)
        mean = jnp.where(
            iota((128 * packed, 128), 1) == (src >> 7) * width + ((src & 127) >> level), 1.0 / packed, 0.0
        ).astype(BF16)
        first = FIRST[level]
        for g in range(8 // packed):
            cols = slice(g * packed * 128, (g + 1) * packed * 128)
            value = dot(cal[first : first + SIZES[level], cols], mean)
            for u in range(SIZES[level] // 32):
                row = UNIT_ROW[first // 32 + u] + g
                wide[pl.ds(row, 32, ROWS), :] = value[u * 32 : (u + 1) * 32]
    for row in range(44, ROWS):
        wide[pl.ds(row, 32, ROWS), :] = jnp.zeros((32, 128), F32)
    for m in range(32):
        out_ref[m, 0:ROWS, :] = wide[m * ROWS : (m + 1) * ROWS, :].astype(BF16)

    for level in (1, 2):
        group = iota((256, 256), 0) >> level == iota((256, 256), 1) >> level
        mean = jnp.where(group, 0.5**level, 0.0).astype(BF16)
        rows = slice(FIRST[level], FIRST[level] + SIZES[level])
        for c in range(0, 8, 2):
            cols = slice(c * 128, (c + 2) * 128)
            cal[rows, cols] = dot(cal[rows, cols], mean).astype(BF16)
    low = low_lanes(256)
    for g in range(4):
        block_cols = cal[:, g * 256 : (g + 1) * 256]
        even = dot(weight_ref[0], block_cols)
        odd = dot(weight_ref[1], block_cols)
        part = jnp.where(
            low, even[:, lanes(0)] + roll64(odd[:, lanes(0)]), roll64(even[:, lanes(1)]) + odd[:, lanes(1)]
        ).astype(BF16)
        for m in range(32):
            row = ROWS + g * 8
            out_ref[m, row : row + 8, :] = part[m * 8 : (m + 1) * 8, :]


def calibrate(me, gains, left, right, weight, vis, x, z, xz):
    vmem = pl.BlockSpec(memory_space=pltpu.VMEM)
    return pl.pallas_call(
        calibrate_kernel,
        in_specs=[pl.BlockSpec(memory_space=pltpu.SMEM)] + [vmem] * 8,
        out_specs=vmem,
        out_shape=jax.ShapeDtypeStruct((32, ROWS + 32, 128), BF16),
        scratch_shapes=[
            pltpu.VMEM((256, 1024), F32),
            pltpu.VMEM((KEEP, 1024), F32),
            pltpu.VMEM((KEEP, 1024), F32),
            pltpu.VMEM((KEEP, 1024), BF16),
            pltpu.VMEM((32 * ROWS, 128), F32),
        ],
        compiler_params=pltpu.CompilerParams(vmem_limit_bytes=VMEM_LIMIT),
        name="calibrate",
    )(me, gains, left, right, weight, vis, x, z, xz)


def finish_kernel(recv_ref, pick_ref, lane_ref, time_ref, avg_ref, grid_ref, means):
    for t in range(32):
        means[t, 0:16, :] = recv_ref[t, 0:16, :].astype(F32)
    for side in range(2):
        for r in range(16, ROWS, 8):
            row = r + 32 * side
            level = time_ref[row : row + 8, :]
            at_least = [level >= 2.0, level >= 3.0]
            for x in range(0, 32, 8):
                two = [recv_ref[x + 2 * j + side, r : r + 8, :].astype(F32) for j in range(4)]
                four = [0.5 * (two[2 * j] + two[2 * j + 1]) for j in range(2)]
                eight = 0.5 * (four[0] + four[1])
                top = [jnp.where(at_least[1], eight, four[j]) for j in range(2)]
                for j in range(4):
                    value = jnp.where(at_least[0], top[j // 2], two[j])
                    means[x + 2 * j, row : row + 8, :] = value
                    means[x + 2 * j + 1, row : row + 8, :] = value

    pick = pick_ref[:, 0:MEANS]
    index = [lane_ref[0], lane_ref[1]]
    low = low_lanes(128)

    def step(i, carry):
        first = (i >> 3) * 16 + (i & 7)
        both = jnp.concatenate([means[first], means[first + 8]], axis=1).astype(BF16)
        rows = dot(pick, both)
        for bit in range(2):
            half = [
                jnp.take_along_axis(rows[:, lanes(k)], index[bit], axis=1, mode="promise_in_bounds") for k in range(2)
            ]
            avg_ref[first + 8 * bit] = jnp.where(low, half[0], half[1]).astype(BF16).reshape(8, 16, 128)
        return carry

    lax.fori_loop(0, 16, step, 0, unroll=8)

    low8 = low_lanes(8)
    for g in range(4):
        row = ROWS + g * 8
        total = []
        for half in range(2):
            sources = [x * 8 + z for x in (half, half + 2) for z in range(8)]
            value = recv_ref[sources[0], row : row + 8, :].astype(F32)
            for source in sources[1:]:
                value = value + recv_ref[source, row : row + 8, :].astype(F32)
            total.append(value)
        even = jnp.where(low8, total[0], roll64(total[1]))
        odd = jnp.where(low8, roll64(total[0]), total[1])
        for u in range(8):
            grid_ref[u, 2 * g : 2 * g + 1, :] = even[u : u + 1, :]
            grid_ref[u, 2 * g + 1 : 2 * g + 2, :] = odd[u : u + 1, :]


def finish(recv, pick, lane, time):
    vmem = pl.BlockSpec(memory_space=pltpu.VMEM)
    return pl.pallas_call(
        finish_kernel,
        in_specs=[vmem] * 4,
        out_specs=[vmem] * 2,
        out_shape=[
            jax.ShapeDtypeStruct((32, 8, 16, 128), BF16),
            jax.ShapeDtypeStruct((8, 8, 128), F32),
        ],
        scratch_shapes=[pltpu.VMEM((32, MEANS, 128), F32)],
        compiler_params=pltpu.CompilerParams(vmem_limit_bytes=VMEM_LIMIT),
        name="finish",
    )(recv, pick, lane, time)


def shards(visibilities, station_gains, station_pairs, average_bands, tile_map, baseline_order):
    me = lax.axis_index("tm").reshape(1)
    bands = average_bands.T
    keep, x, z, xz, hot, position = route(me, bands, baseline_order[None, :], visibilities[0])
    x, z, xz = [
        lax.ppermute(value, "tm", [(m, m ^ bits) for m in range(32)]) for value, bits in ((x, 8), (z, 1), (xz, 9))
    ]
    gains = lax.all_to_all(cut_gains(me, station_gains, position), "chan", 0, 0, tiled=True)
    left, right, weight, pick, lane, time = tables(me, station_pairs.T, bands, tile_map.T, hot, position)
    payload = calibrate(me, gains, left, right, weight, keep, x, z, xz)
    recv = lax.all_to_all(payload, "tm", 0, 0, tiled=True)
    averaged, gridded = finish(recv, pick, lane, time)
    return averaged, gridded


def solution(mesh):
    return jax.shard_map(
        shards,
        mesh=mesh,
        in_specs=(P("tm", None, None, "chan"), P(None, "chan", None), P(), P(), P(), P()),
        out_specs=(P(None, None, "tm", "chan"), P("tm", None, "chan")),
        check_vma=False,
    )
```

```python
import functools
import jax
import jax.numpy as jnp
from jax import lax
from jax.experimental import pallas as pl
from jax.experimental.pallas import tpu as pltpu
from jax.sharding import PartitionSpec as P

KEEP = 320
SEND = 192
STACK = 384
FIRST = (0, 96, 192)
SIZES = (96, 96, 128)
UNIT_ROW = (0, 16, 24, 8, 32, 36, 12, 14, 40, 42)
ROWS = 48
MEANS = 80
F32 = jnp.float32
BF16 = jnp.bfloat16
VMEM_LIMIT = 24 << 20


def iota(shape, axis):
    return lax.broadcasted_iota(jnp.int32, shape, axis)


def one_hot(mask):
    return jnp.where(mask, 1.0, 0.0).astype(BF16)


def dot(a, b):
    return lax.dot_general(a, b, (((1,), (0,)), ((), ())), preferred_element_type=F32)


def dot_t(a, b):
    return lax.dot_general(a, b, (((1,), (1,)), ((), ())), preferred_element_type=F32)


def roll64(value):
    return pltpu.roll(value, 64, 1)


def low_lanes(rows):
    return iota((rows, 128), 1) < 64


def rows_of(values, width):
    row = iota((8, width), 0)
    result = jnp.zeros((8, width), F32)
    for i, value in enumerate(values):
        result = jnp.where(row == i, value, result)
    return result


def gains_kernel(me_ref, gain_ref, after_ref, out_ref):
    del after_ref
    first_half = ((me_ref[0] >> 3) & 1) == 0
    stations = gain_ref.shape[1]
    low = low_lanes(stations)
    for d in range(8):
        for g in range(4):
            a = gain_ref[2 * g, :, d * 128 : (d + 1) * 128]
            b = gain_ref[2 * g + 1, :, d * 128 : (d + 1) * 128]
            a = jnp.where(first_half, a, roll64(a))
            b = jnp.where(first_half, roll64(b), b)
            out_ref[d, g * stations : (g + 1) * stations, :] = jnp.where(low, a, b).astype(BF16)


def cut_gains(me, gains, after):
    comps, stations, _ = gains.shape
    return pl.pallas_call(
        gains_kernel,
        in_specs=[
            pl.BlockSpec(memory_space=pltpu.SMEM),
            pl.BlockSpec(memory_space=pltpu.VMEM),
            pl.BlockSpec(memory_space=pl.ANY),
        ],
        out_shape=jax.ShapeDtypeStruct((8, comps // 2 * stations, 128), BF16),
        compiler_params=pltpu.CompilerParams(vmem_limit_bytes=VMEM_LIMIT),
        name="cut_gains",
    )(me, gains, after)


def slots_kernel(me_ref, bands_ref, order_ref, hot_out, position_out):
    me = me_ref[0]
    nb = order_ref.shape[1]
    info = rows_of([bands_ref[0:1, :].astype(F32), bands_ref[1:2, :].astype(F32)], nb).astype(BF16)
    order_hot = one_hot(iota((nb, nb), 0) == order_ref[...])
    at_position = dot(info, order_hot)
    time_here = at_position[0:1, :]
    chan_here = at_position[1:2, :].astype(jnp.int32)
    kind = jnp.where(time_here == 0.0, 0, 3) + chan_here
    same = rows_of([jnp.where(kind == i, 1.0, 0.0) for i in range(6)], nb)
    before = one_hot(
        (iota((nb, nb), 0) < iota((nb, nb), 1)) & ((iota((nb, nb), 0) >> 4) == (iota((nb, nb), 1) >> 4))
    )
    counts = dot(same.astype(BF16), before)
    count = counts[0:1, :]
    for i in range(1, 6):
        count = jnp.where(kind == i, counts[i : i + 1, :], count)
    count = count.astype(jnp.int32)
    side = jnp.where(kind < 3, 0, count >> 1)
    place = jnp.where(kind < 3, count, count & 1)
    kept = jnp.where(chan_here == 0, 1, jnp.where(chan_here == 1, 4, 8)) + place
    sent = 10 + 2 * chan_here + place
    single = jnp.where(chan_here == 0, 0, jnp.where(chan_here == 1, 3, 6)) + place
    unit = jnp.where(kind < 3, single, jnp.where(side == (me & 1), kept, sent))
    slot = unit * 32 + (iota((1, nb), 1) >> 4)
    hot_out[...] = dot_t(one_hot(iota((nb, nb), 0) == slot), order_hot).astype(BF16)
    position_out[...] = rows_of(
        [time_here, chan_here.astype(F32), kind.astype(F32), side.astype(F32), place.astype(F32)], nb
    )


def slots(me, bands, order):
    nb = order.shape[1]
    vmem = pl.BlockSpec(memory_space=pltpu.VMEM)
    return pl.pallas_call(
        slots_kernel,
        in_specs=[pl.BlockSpec(memory_space=pltpu.SMEM), vmem, vmem],
        out_shape=[jax.ShapeDtypeStruct((nb, nb), BF16), jax.ShapeDtypeStruct((8, nb), F32)],
        compiler_params=pltpu.CompilerParams(vmem_limit_bytes=VMEM_LIMIT),
        cost_estimate=pl.CostEstimate(flops=1_000_000_000, bytes_accessed=3_000_000, transcendentals=0),
        name="slots",
    )(me, bands, order)


def route_kernel(me_ref, hot_ref, vis_ref, keep_out, x_out, z_out, xz_out):
    me = me_ref[0]
    slot_hot = hot_ref[...]
    nb = slot_hot.shape[0]
    mine = low_lanes(nb) == (((me >> 3) & 1) == 0)
    for g in range(4):
        both = jnp.concatenate([vis_ref[2 * g], vis_ref[2 * g + 1]], axis=1)
        moved = dot(slot_hot, both)
        a = moved[:, lanes(0)]
        b = moved[:, lanes(1)]
        keep_out[2 * g] = a[:KEEP].astype(BF16)
        keep_out[2 * g + 1] = b[:KEEP].astype(BF16)
        there = jnp.where(mine, roll64(a), b).astype(BF16)
        x_out[g] = there[:KEEP]
        xz_out[g] = there[KEEP:]
        z_out[g] = jnp.where(mine[KEEP:], a[KEEP:], roll64(b[KEEP:])).astype(BF16)


def route(me, hot, vis):
    vmem = pl.BlockSpec(memory_space=pltpu.VMEM)
    return pl.pallas_call(
        route_kernel,
        in_specs=[pl.BlockSpec(memory_space=pltpu.SMEM), vmem, vmem],
        out_shape=[
            jax.ShapeDtypeStruct((8, KEEP, 128), BF16),
            jax.ShapeDtypeStruct((4, KEEP, 128), BF16),
            jax.ShapeDtypeStruct((4, SEND, 128), BF16),
            jax.ShapeDtypeStruct((4, SEND, 128), BF16),
        ],
        compiler_params=pltpu.CompilerParams(vmem_limit_bytes=VMEM_LIMIT),
        name="route",
    )(me, hot, vis)


def tables_kernel(
    me_ref, pairs_ref, bands_ref, tiles_ref, hot_ref, position_ref,
    left_out, right_out, weight_out, pick_out, lane_out, time_out,
):
    me = me_ref[0]
    nb = pairs_ref.shape[1]
    time_level = bands_ref[0:1, :]
    tiles = []
    for now in (me & ~8, me | 8):
        tile = tiles_ref[pl.ds(now, 1), :]
        for level in range(1, 4):
            start = (now >> level) << level
            tile = jnp.where(time_level == level, tiles_ref[pl.ds(start, 1), :], tile)
        tiles.append(tile.astype(F32))
    info = rows_of([time_level.astype(F32)] + tiles, nb).astype(BF16)
    slot_hot = hot_ref[0:KEEP, :]
    left_out[...] = dot_t(slot_hot, one_hot(iota((256, nb), 0) == pairs_ref[0:1, :])).astype(BF16)
    right_out[...] = dot_t(slot_hot, one_hot(iota((256, nb), 0) == pairs_ref[1:2, :])).astype(BF16)

    at_slot = dot_t(info, slot_hot)
    time_slot = at_slot[0:1, :]
    weight = jnp.where(time_slot <= 1.0, 1.0, jnp.where(time_slot == 2.0, 0.5, 0.25))
    weight_out[...] = jnp.zeros((256, 2 * STACK), BF16)
    for i in range(2):
        tile_slot = at_slot[1 + i : 2 + i, :].astype(jnp.int32)
        weight_out[:, i * STACK : i * STACK + KEEP] = jnp.where(iota((256, KEEP), 0) == tile_slot, weight, 0.0).astype(BF16)

    own = dot(
        position_ref[...].astype(BF16), one_hot(iota((nb, 128), 0) == me * 16 + (iota((nb, 128), 1) & 15))
    )
    own_time = own[0:1, :]
    own_chan = own[1:2, :].astype(jnp.int32)
    own_kind = own[2:3, :].astype(jnp.int32)
    own_side = own[3:4, :].astype(jnp.int32)
    own_place = own[4:5, :].astype(jnp.int32)
    comp = iota((1, 128), 1) >> 4
    within = jnp.where(
        own_chan == 0,
        own_place * 8 + comp,
        jnp.where(own_chan == 1, own_place * 4 + (comp >> 1), own_place * 2 + (comp >> 2)),
    )
    single = jnp.where(own_chan == 0, 0, jnp.where(own_chan == 1, 8, 12))
    sided = 16 + 32 * own_side + jnp.where(own_chan == 0, 0, jnp.where(own_chan == 1, 16, 24))
    packed_row = jnp.where(own_kind < 3, single, sided) + within
    part = jnp.where(own_chan == 0, 0, jnp.where(own_chan == 1, 1 + (comp & 1), 3 + (comp & 3)))
    sub = iota((128, 128), 0)
    lan = iota((128, 128), 1)
    eye = one_hot(sub == lan)
    row_hot = one_hot(sub == packed_row)
    pick_out[...] = dot_t(eye, row_hot).astype(BF16)
    part_hot = dot_t(eye, one_hot(sub == part)).astype(BF16)
    inside = lan & 63
    for bit in range(2):
        table = jnp.where(
            sub == 0,
            bit * 64 + inside,
            jnp.where(
                sub <= 2,
                (sub - 1) * 64 + bit * 32 + (inside >> 1),
                jnp.where(sub <= 6, (sub - 3) * 32 + bit * 16 + (inside >> 2), 0),
            ),
        )
        lane_out[bit] = dot(part_hot, table.astype(F32).astype(BF16)).astype(jnp.int32)
    inner = (sub - 16) & 31
    level_of = jnp.where(sub < 8, 0, jnp.where(sub < 12, 1, 2))
    level_of = jnp.where(sub < 16, level_of, jnp.where(inner < 16, 0, jnp.where(inner < 24, 1, 2)))
    share = jnp.where(level_of == 0, 1.0, jnp.where(level_of == 1, 0.5, 0.25))
    spread = jnp.broadcast_to(own_time, (128, 128)).astype(BF16)
    time_out[...] = dot_t(row_hot, spread) * share


def tables(me, pairs, bands, tiles, hot, position):
    vmem = pl.BlockSpec(memory_space=pltpu.VMEM)
    nb = pairs.shape[1]
    return pl.pallas_call(
        tables_kernel,
        in_specs=[pl.BlockSpec(memory_space=pltpu.SMEM)] + [vmem] * 5,
        out_shape=[
            jax.ShapeDtypeStruct((KEEP, 256), BF16),
            jax.ShapeDtypeStruct((KEEP, 256), BF16),
            jax.ShapeDtypeStruct((256, 2 * STACK), BF16),
            jax.ShapeDtypeStruct((128, 128), BF16),
            jax.ShapeDtypeStruct((2, 128, 128), jnp.int32),
            jax.ShapeDtypeStruct((128, 128), F32),
        ],
        compiler_params=pltpu.CompilerParams(vmem_limit_bytes=VMEM_LIMIT),
        cost_estimate=pl.CostEstimate(flops=1_000_000_000, bytes_accessed=4_000_000, transcendentals=0),
        name="tables",
    )(me, pairs, bands, tiles, hot, position)


def product(left, right):
    return (left[0] * right[0] - left[1] * right[1], left[0] * right[1] + left[1] * right[0])


def product_conj(left, right):
    return (left[0] * right[0] + left[1] * right[1], left[1] * right[0] - left[0] * right[1])


def add_pair(left, right):
    return (left[0] + right[0], left[1] + right[1])


def as_matrix(components):
    return [
        [(components[0], components[1]), (components[2], components[3])],
        [(components[4], components[5]), (components[6], components[7])],
    ]


def jones_apply(first, middle, second):
    left_gain = as_matrix(first)
    coherency = as_matrix(middle)
    right_gain = as_matrix(second)
    partial_rows = [
        [
            add_pair(
                product(left_gain[i][0], coherency[0][k]), product(left_gain[i][1], coherency[1][k])
            )
            for k in range(2)
        ]
        for i in range(2)
    ]
    result = []
    for i in range(2):
        for c in range(2):
            element = add_pair(
                product_conj(partial_rows[i][0], right_gain[c][0]),
                product_conj(partial_rows[i][1], right_gain[c][1]),
            )
            result.extend(element)
    return result


def lanes(c):
    return slice(c * 128, (c + 1) * 128)


def calibrate_kernel(
    me_ref, gain_ref, left_ref, right_ref, weight_ref, vis_ref, x_ref, z_ref, xz_ref, out_ref, gains, gl, gr, cal, wide, stack
):
    stations = gain_ref.shape[1] // 4
    low = low_lanes(stations)
    for d in range(8):
        for g in range(4):
            both = gain_ref[d, g * stations : (g + 1) * stations, :].astype(F32)
            swapped = roll64(both)
            gains[d * stations : (d + 1) * stations, lanes(2 * g)] = jnp.where(low, both, swapped)
            gains[d * stations : (d + 1) * stations, lanes(2 * g + 1)] = jnp.where(low, swapped, both)
    gains[8 * stations :, :] = jnp.zeros((256 - 8 * stations, 1024), F32)
    table = gains[...].astype(BF16)
    gl[...] = dot(left_ref[...], table)
    gr[...] = dot(right_ref[...], table)

    mine = low_lanes(16) == (((me_ref[0] >> 3) & 1) == 0)

    def spread(ref, g, rows):
        both = ref[g, rows, :].astype(F32)
        return both, roll64(both)

    def stack_rows(g, start, rows, a, b):
        low = low_lanes(a.shape[0])
        stack[pl.ds(start, rows), lanes(g)] = jnp.where(low, a, roll64(b)).astype(BF16)
        stack[pl.ds(STACK + start, rows), lanes(g)] = jnp.where(low, roll64(a), b).astype(BF16)

    for part in (KEEP, STACK + KEEP):
        stack[part : part + STACK - KEEP, :] = jnp.zeros((STACK - KEEP, 512), BF16)

    def block(first, other, level):
        rows = pl.ds(pl.multiple_of(first, 16), 16)
        value = []
        for g in range(4):
            theirs = spread(x_ref, g, rows)
            pair = [jnp.where(mine, vis_ref[2 * g + i, rows, :].astype(F32), theirs[i]) for i in range(2)]
            if other is not None:
                near = spread(z_ref, g, other)
                far = spread(xz_ref, g, other)
                pair = [0.5 * (pair[i] + jnp.where(mine, near[i], far[i])) for i in range(2)]
            value.extend(pair)
        result = jones_apply(
            [gl[rows, lanes(c)] for c in range(8)], value, [gr[rows, lanes(c)] for c in range(8)]
        )
        for c in range(8):
            cal[rows, lanes(c)] = result[c].astype(BF16)
        if level == 0:
            for g in range(4):
                stack_rows(g, pl.multiple_of(first, 16), 16, result[2 * g], result[2 * g + 1])

    for level, singles in ((0, 32), (1, 32), (2, 64)):

        def single(i, carry, level=level):
            block(FIRST[level] + i * 16, None, level)
            return carry

        def paired(i, carry, level=level, singles=singles):
            other = pl.ds(pl.multiple_of(level * 64 + i * 16, 16), 16)
            block(FIRST[level] + singles + i * 16, other, level)
            return carry

        lax.fori_loop(0, singles // 16, single, 0, unroll=2)
        lax.fori_loop(0, 4, paired, 0, unroll=4)

    for u in range(3):
        for c in range(8):
            wide[pl.ds(UNIT_ROW[u] + c, 32, ROWS), :] = cal[u * 32 : (u + 1) * 32, lanes(c)].astype(F32)
    for level in (1, 2):
        packed = 1 << level
        width = 128 >> level
        src = iota((128 * packed, 128), 0)
        mean = jnp.where(
            iota((128 * packed, 128), 1) == (src >> 7) * width + ((src & 127) >> level), 1.0 / packed, 0.0
        ).astype(BF16)
        first = FIRST[level]
        for g in range(8 // packed):
            cols = slice(g * packed * 128, (g + 1) * packed * 128)
            value = dot(cal[first : first + SIZES[level], cols], mean)
            for u in range(SIZES[level] // 32):
                row = UNIT_ROW[first // 32 + u] + g
                wide[pl.ds(row, 32, ROWS), :] = value[u * 32 : (u + 1) * 32]
    for row in range(44, ROWS):
        wide[pl.ds(row, 32, ROWS), :] = jnp.zeros((32, 128), F32)
    for m in range(32):
        out_ref[m, 0:ROWS, :] = wide[m * ROWS : (m + 1) * ROWS, :].astype(BF16)

    for level in (1, 2):
        group = iota((256, 256), 0) >> level == iota((256, 256), 1) >> level
        mean = jnp.where(group, 0.5**level, 0.0).astype(BF16)
        rows = slice(FIRST[level], FIRST[level] + SIZES[level])
        for g in range(4):
            value = dot(cal[rows, g * 256 : (g + 1) * 256], mean)
            stack_rows(g, FIRST[level], SIZES[level], value[:, lanes(0)], value[:, lanes(1)])
    for g in range(0, 4, 2):
        part = dot(weight_ref[...], stack[:, g * 128 : (g + 2) * 128]).astype(BF16)
        for m in range(32):
            for i in range(2):
                row = ROWS + (g + i) * 8
                out_ref[m, row : row + 8, :] = part[m * 8 : (m + 1) * 8, lanes(i)]


def calibrate(me, gains, left, right, weight, vis, x, z, xz):
    vmem = pl.BlockSpec(memory_space=pltpu.VMEM)
    return pl.pallas_call(
        calibrate_kernel,
        in_specs=[pl.BlockSpec(memory_space=pltpu.SMEM)] + [vmem] * 8,
        out_specs=vmem,
        out_shape=jax.ShapeDtypeStruct((32, ROWS + 32, 128), BF16),
        scratch_shapes=[
            pltpu.VMEM((256, 1024), F32),
            pltpu.VMEM((KEEP, 1024), F32),
            pltpu.VMEM((KEEP, 1024), F32),
            pltpu.VMEM((KEEP, 1024), BF16),
            pltpu.VMEM((32 * ROWS, 128), F32),
            pltpu.VMEM((2 * STACK, 512), BF16),
        ],
        compiler_params=pltpu.CompilerParams(vmem_limit_bytes=VMEM_LIMIT),
        name="calibrate",
    )(me, gains, left, right, weight, vis, x, z, xz)


def finish_kernel(recv_ref, pick_ref, lane_ref, time_ref, avg_ref, grid_ref, means):
    for t in range(32):
        means[t, 0:16, :] = recv_ref[t, 0:16, :].astype(F32)
    for side in range(2):
        for r in range(16, ROWS, 8):
            row = r + 32 * side
            level = time_ref[row : row + 8, :]
            at_least = [level >= 2.0, level >= 3.0]
            for x in range(0, 32, 8):
                two = [recv_ref[x + 2 * j + side, r : r + 8, :].astype(F32) for j in range(4)]
                four = [0.5 * (two[2 * j] + two[2 * j + 1]) for j in range(2)]
                eight = 0.5 * (four[0] + four[1])
                top = [jnp.where(at_least[1], eight, four[j]) for j in range(2)]
                for j in range(4):
                    value = jnp.where(at_least[0], top[j // 2], two[j])
                    means[x + 2 * j, row : row + 8, :] = value
                    means[x + 2 * j + 1, row : row + 8, :] = value

    pick = pick_ref[:, 0:MEANS]
    index = [lane_ref[0], lane_ref[1]]
    low = low_lanes(128)

    def step(i, carry):
        first = (i >> 3) * 16 + (i & 7)
        both = jnp.concatenate([means[first], means[first + 8]], axis=1).astype(BF16)
        rows = dot(pick, both)
        for bit in range(2):
            half = [
                jnp.take_along_axis(rows[:, lanes(k)], index[bit], axis=1, mode="promise_in_bounds") for k in range(2)
            ]
            avg_ref[first + 8 * bit] = jnp.where(low, half[0], half[1]).astype(BF16).reshape(8, 16, 128)
        return carry

    lax.fori_loop(0, 16, step, 0, unroll=8)

    low8 = low_lanes(8)
    for g in range(4):
        row = ROWS + g * 8
        total = []
        for half in range(2):
            sources = [x * 8 + z for x in (half, half + 2) for z in range(8)]
            value = recv_ref[sources[0], row : row + 8, :].astype(F32)
            for source in sources[1:]:
                value = value + recv_ref[source, row : row + 8, :].astype(F32)
            total.append(value)
        even = jnp.where(low8, total[0], roll64(total[1]))
        odd = jnp.where(low8, roll64(total[0]), total[1])
        for u in range(8):
            grid_ref[u, 2 * g : 2 * g + 1, :] = even[u : u + 1, :]
            grid_ref[u, 2 * g + 1 : 2 * g + 2, :] = odd[u : u + 1, :]


def finish(recv, pick, lane, time):
    vmem = pl.BlockSpec(memory_space=pltpu.VMEM)
    return pl.pallas_call(
        finish_kernel,
        in_specs=[vmem] * 4,
        out_specs=[vmem] * 2,
        out_shape=[
            jax.ShapeDtypeStruct((32, 8, 16, 128), BF16),
            jax.ShapeDtypeStruct((8, 8, 128), F32),
        ],
        scratch_shapes=[pltpu.VMEM((32, MEANS, 128), F32)],
        compiler_params=pltpu.CompilerParams(vmem_limit_bytes=VMEM_LIMIT),
        name="finish",
    )(recv, pick, lane, time)


def shards(visibilities, station_gains, station_pairs, average_bands, tile_map, baseline_order):
    me = lax.axis_index("tm").reshape(1)
    bands = average_bands.T
    hot, position = slots(me, bands, baseline_order[None, :])
    keep, x, z, xz = route(me, hot, visibilities[0])
    x, z, xz = [
        lax.ppermute(value, "tm", [(m, m ^ bits) for m in range(32)]) for value, bits in ((x, 8), (z, 1), (xz, 9))
    ]
    gains = lax.all_to_all(cut_gains(me, station_gains, keep), "chan", 0, 0, tiled=True)
    left, right, weight, pick, lane, time = tables(me, station_pairs.T, bands, tile_map.T, hot, position)
    payload = calibrate(me, gains, left, right, weight, keep, x, z, xz)
    recv = lax.all_to_all(payload, "tm", 0, 0, tiled=True)
    averaged, gridded = finish(recv, pick, lane, time)
    return averaged, gridded


def solution(mesh):
    return jax.shard_map(
        shards,
        mesh=mesh,
        in_specs=(P("tm", None, None, "chan"), P(None, "chan", None), P(), P(), P(), P()),
        out_specs=(P(None, None, "tm", "chan"), P("tm", None, "chan")),
        check_vma=False,
    )
```

```python
import functools
import jax
import jax.numpy as jnp
from jax import lax
from jax.experimental import pallas as pl
from jax.experimental.pallas import tpu as pltpu
from jax.sharding import PartitionSpec as P

KEEP = 320
SEND = 192
STACK = 384
FIRST = (0, 96, 192)
SIZES = (96, 96, 128)
UNIT_ROW = (0, 16, 24, 8, 32, 36, 12, 14, 40, 42)
ROWS = 48
MEANS = 80
F32 = jnp.float32
BF16 = jnp.bfloat16
VMEM_LIMIT = 24 << 20


def iota(shape, axis):
    return lax.broadcasted_iota(jnp.int32, shape, axis)


def one_hot(mask):
    return jnp.where(mask, 1.0, 0.0).astype(BF16)


def dot(a, b):
    return lax.dot_general(a, b, (((1,), (0,)), ((), ())), preferred_element_type=F32)


def dot_t(a, b):
    return lax.dot_general(a, b, (((1,), (1,)), ((), ())), preferred_element_type=F32)


def roll64(value):
    return pltpu.roll(value, 64, 1)


def low_lanes(rows):
    return iota((rows, 128), 1) < 64


def rows_of(values, width):
    row = iota((8, width), 0)
    result = jnp.zeros((8, width), F32)
    for i, value in enumerate(values):
        result = jnp.where(row == i, value, result)
    return result


def gains_kernel(me_ref, gain_ref, after_ref, out_ref):
    del after_ref
    first_half = ((me_ref[0] >> 3) & 1) == 0
    stations = gain_ref.shape[1]
    low = low_lanes(stations)
    for d in range(8):
        for g in range(4):
            a = gain_ref[2 * g, :, d * 128 : (d + 1) * 128]
            b = gain_ref[2 * g + 1, :, d * 128 : (d + 1) * 128]
            a = jnp.where(first_half, a, roll64(a))
            b = jnp.where(first_half, roll64(b), b)
            out_ref[d, g * stations : (g + 1) * stations, :] = jnp.where(low, a, b).astype(BF16)


def cut_gains(me, gains, after):
    comps, stations, _ = gains.shape
    return pl.pallas_call(
        gains_kernel,
        in_specs=[
            pl.BlockSpec(memory_space=pltpu.SMEM),
            pl.BlockSpec(memory_space=pltpu.VMEM),
            pl.BlockSpec(memory_space=pl.ANY),
        ],
        out_shape=jax.ShapeDtypeStruct((8, comps // 2 * stations, 128), BF16),
        compiler_params=pltpu.CompilerParams(vmem_limit_bytes=VMEM_LIMIT),
        name="cut_gains",
    )(me, gains, after)


def slots_kernel(me_ref, bands_ref, order_ref, hot_out, position_out):
    me = me_ref[0]
    nb = order_ref.shape[1]
    info = rows_of([bands_ref[0:1, :].astype(F32), bands_ref[1:2, :].astype(F32)], nb).astype(BF16)
    order_hot = one_hot(iota((nb, nb), 0) == order_ref[...])
    at_position = dot(info, order_hot)
    time_here = at_position[0:1, :]
    chan_here = at_position[1:2, :].astype(jnp.int32)
    kind = jnp.where(time_here == 0.0, 0, 3) + chan_here
    same = rows_of([jnp.where(kind == i, 1.0, 0.0) for i in range(6)], nb)
    before = one_hot(
        (iota((nb, nb), 0) < iota((nb, nb), 1)) & ((iota((nb, nb), 0) >> 4) == (iota((nb, nb), 1) >> 4))
    )
    counts = dot(same.astype(BF16), before)
    count = counts[0:1, :]
    for i in range(1, 6):
        count = jnp.where(kind == i, counts[i : i + 1, :], count)
    count = count.astype(jnp.int32)
    side = jnp.where(kind < 3, 0, count >> 1)
    place = jnp.where(kind < 3, count, count & 1)
    kept = jnp.where(chan_here == 0, 1, jnp.where(chan_here == 1, 4, 8)) + place
    sent = 10 + 2 * chan_here + place
    single = jnp.where(chan_here == 0, 0, jnp.where(chan_here == 1, 3, 6)) + place
    unit = jnp.where(kind < 3, single, jnp.where(side == (me & 1), kept, sent))
    slot = unit * 32 + (iota((1, nb), 1) >> 4)
    hot_out[...] = dot_t(one_hot(iota((nb, nb), 0) == slot), order_hot).astype(BF16)
    position_out[...] = rows_of(
        [time_here, chan_here.astype(F32), kind.astype(F32), side.astype(F32), place.astype(F32)], nb
    )


def slots(me, bands, order):
    nb = order.shape[1]
    vmem = pl.BlockSpec(memory_space=pltpu.VMEM)
    return pl.pallas_call(
        slots_kernel,
        in_specs=[pl.BlockSpec(memory_space=pltpu.SMEM), vmem, vmem],
        out_shape=[jax.ShapeDtypeStruct((nb, nb), BF16), jax.ShapeDtypeStruct((8, nb), F32)],
        compiler_params=pltpu.CompilerParams(vmem_limit_bytes=VMEM_LIMIT),
        cost_estimate=pl.CostEstimate(flops=1_000_000_000, bytes_accessed=3_000_000, transcendentals=0),
        name="slots",
    )(me, bands, order)


def route_kernel(me_ref, hot_ref, vis_ref, keep_out, x_out, z_out, xz_out):
    me = me_ref[0]
    slot_hot = hot_ref[...]
    nb = slot_hot.shape[0]
    mine = low_lanes(nb) == (((me >> 3) & 1) == 0)
    for g in range(4):
        both = jnp.concatenate([vis_ref[2 * g], vis_ref[2 * g + 1]], axis=1)
        moved = dot(slot_hot, both)
        a = moved[:, lanes(0)]
        b = moved[:, lanes(1)]
        keep_out[2 * g] = a[:KEEP].astype(BF16)
        keep_out[2 * g + 1] = b[:KEEP].astype(BF16)
        there = jnp.where(mine, roll64(a), b).astype(BF16)
        x_out[g] = there[:KEEP]
        xz_out[g] = there[KEEP:]
        z_out[g] = jnp.where(mine[KEEP:], a[KEEP:], roll64(b[KEEP:])).astype(BF16)


def route(me, hot, vis):
    vmem = pl.BlockSpec(memory_space=pltpu.VMEM)
    return pl.pallas_call(
        route_kernel,
        in_specs=[pl.BlockSpec(memory_space=pltpu.SMEM), vmem, vmem],
        out_shape=[
            jax.ShapeDtypeStruct((8, KEEP, 128), BF16),
            jax.ShapeDtypeStruct((4, KEEP, 128), BF16),
            jax.ShapeDtypeStruct((4, SEND, 128), BF16),
            jax.ShapeDtypeStruct((4, SEND, 128), BF16),
        ],
        compiler_params=pltpu.CompilerParams(vmem_limit_bytes=VMEM_LIMIT),
        name="route",
    )(me, hot, vis)


def tables_kernel(
    me_ref, pairs_ref, bands_ref, tiles_ref, hot_ref, position_ref,
    left_out, right_out, weight_out, pick_out, lane_out, time_out,
):
    me = me_ref[0]
    nb = pairs_ref.shape[1]
    time_level = bands_ref[0:1, :]
    tiles = []
    for now in (me & ~8, me | 8):
        tile = tiles_ref[pl.ds(now, 1), :]
        for level in range(1, 4):
            start = (now >> level) << level
            tile = jnp.where(time_level == level, tiles_ref[pl.ds(start, 1), :], tile)
        tiles.append(tile.astype(F32))
    info = rows_of([time_level.astype(F32)] + tiles, nb).astype(BF16)
    slot_hot = hot_ref[0:KEEP, :]
    left_out[...] = dot_t(slot_hot, one_hot(iota((256, nb), 0) == pairs_ref[0:1, :])).astype(BF16)
    right_out[...] = dot_t(slot_hot, one_hot(iota((256, nb), 0) == pairs_ref[1:2, :])).astype(BF16)

    at_slot = dot_t(info, slot_hot)
    time_slot = at_slot[0:1, :]
    weight = jnp.where(time_slot <= 1.0, 1.0, jnp.where(time_slot == 2.0, 0.5, 0.25))
    weight_out[...] = jnp.zeros((256, 2 * STACK), BF16)
    for i in range(2):
        tile_slot = at_slot[1 + i : 2 + i, :].astype(jnp.int32)
        weight_out[:, i * STACK : i * STACK + KEEP] = jnp.where(iota((256, KEEP), 0) == tile_slot, weight, 0.0).astype(BF16)

    own = dot(
        position_ref[...].astype(BF16), one_hot(iota((nb, 128), 0) == me * 16 + (iota((nb, 128), 1) & 15))
    )
    own_time = own[0:1, :]
    own_chan = own[1:2, :].astype(jnp.int32)
    own_kind = own[2:3, :].astype(jnp.int32)
    own_side = own[3:4, :].astype(jnp.int32)
    own_place = own[4:5, :].astype(jnp.int32)
    comp = iota((1, 128), 1) >> 4
    within = jnp.where(
        own_chan == 0,
        own_place * 8 + comp,
        jnp.where(own_chan == 1, own_place * 4 + (comp >> 1), own_place * 2 + (comp >> 2)),
    )
    single = jnp.where(own_chan == 0, 0, jnp.where(own_chan == 1, 8, 12))
    sided = 16 + 32 * own_side + jnp.where(own_chan == 0, 0, jnp.where(own_chan == 1, 16, 24))
    packed_row = jnp.where(own_kind < 3, single, sided) + within
    part = jnp.where(own_chan == 0, 0, jnp.where(own_chan == 1, 1 + (comp & 1), 3 + (comp & 3)))
    sub = iota((128, 128), 0)
    lan = iota((128, 128), 1)
    eye = one_hot(sub == lan)
    row_hot = one_hot(sub == packed_row)
    pick_out[...] = dot_t(eye, row_hot).astype(BF16)
    part_hot = dot_t(eye, one_hot(sub == part)).astype(BF16)
    inside = lan & 63
    for bit in range(2):
        table = jnp.where(
            sub == 0,
            bit * 64 + inside,
            jnp.where(
                sub <= 2,
                (sub - 1) * 64 + bit * 32 + (inside >> 1),
                jnp.where(sub <= 6, (sub - 3) * 32 + bit * 16 + (inside >> 2), 0),
            ),
        )
        lane_out[bit] = dot(part_hot, table.astype(F32).astype(BF16)).astype(jnp.int32)
    inner = (sub - 16) & 31
    level_of = jnp.where(sub < 8, 0, jnp.where(sub < 12, 1, 2))
    level_of = jnp.where(sub < 16, level_of, jnp.where(inner < 16, 0, jnp.where(inner < 24, 1, 2)))
    share = jnp.where(level_of == 0, 1.0, jnp.where(level_of == 1, 0.5, 0.25))
    spread = jnp.broadcast_to(own_time, (128, 128)).astype(BF16)
    time_out[...] = dot_t(row_hot, spread) * share


def tables(me, pairs, bands, tiles, hot, position):
    vmem = pl.BlockSpec(memory_space=pltpu.VMEM)
    nb = pairs.shape[1]
    return pl.pallas_call(
        tables_kernel,
        in_specs=[pl.BlockSpec(memory_space=pltpu.SMEM)] + [vmem] * 5,
        out_shape=[
            jax.ShapeDtypeStruct((KEEP, 256), BF16),
            jax.ShapeDtypeStruct((KEEP, 256), BF16),
            jax.ShapeDtypeStruct((256, 2 * STACK), BF16),
            jax.ShapeDtypeStruct((128, 128), BF16),
            jax.ShapeDtypeStruct((2, 128, 128), jnp.int32),
            jax.ShapeDtypeStruct((128, 128), F32),
        ],
        compiler_params=pltpu.CompilerParams(vmem_limit_bytes=VMEM_LIMIT),
        cost_estimate=pl.CostEstimate(flops=1_000_000_000, bytes_accessed=4_000_000, transcendentals=0),
        name="tables",
    )(me, pairs, bands, tiles, hot, position)


def product(left, right):
    return (left[0] * right[0] - left[1] * right[1], left[0] * right[1] + left[1] * right[0])


def product_conj(left, right):
    return (left[0] * right[0] + left[1] * right[1], left[1] * right[0] - left[0] * right[1])


def add_pair(left, right):
    return (left[0] + right[0], left[1] + right[1])


def as_matrix(components):
    return [
        [(components[0], components[1]), (components[2], components[3])],
        [(components[4], components[5]), (components[6], components[7])],
    ]


def jones_apply(first, middle, second):
    left_gain = as_matrix(first)
    coherency = as_matrix(middle)
    right_gain = as_matrix(second)
    partial_rows = [
        [
            add_pair(
                product(left_gain[i][0], coherency[0][k]), product(left_gain[i][1], coherency[1][k])
            )
            for k in range(2)
        ]
        for i in range(2)
    ]
    result = []
    for i in range(2):
        for c in range(2):
            element = add_pair(
                product_conj(partial_rows[i][0], right_gain[c][0]),
                product_conj(partial_rows[i][1], right_gain[c][1]),
            )
            result.extend(element)
    return result


def lanes(c):
    return slice(c * 128, (c + 1) * 128)


def calibrate_kernel(
    me_ref, gain_ref, left_ref, right_ref, weight_ref, vis_ref, x_ref, z_ref, xz_ref, out_ref, gains, gl, gr, cal, wide, stack
):
    stations = gain_ref.shape[1] // 4
    low = low_lanes(stations)
    for d in range(8):
        for g in range(4):
            both = gain_ref[d, g * stations : (g + 1) * stations, :].astype(F32)
            swapped = roll64(both)
            gains[d * stations : (d + 1) * stations, lanes(2 * g)] = jnp.where(low, both, swapped)
            gains[d * stations : (d + 1) * stations, lanes(2 * g + 1)] = jnp.where(low, swapped, both)
    gains[8 * stations :, :] = jnp.zeros((256 - 8 * stations, 1024), F32)
    table = gains[...].astype(BF16)
    gl[...] = dot(left_ref[...], table)
    gr[...] = dot(right_ref[...], table)

    mine = low_lanes(16) == (((me_ref[0] >> 3) & 1) == 0)

    def spread(ref, g, rows):
        both = ref[g, rows, :].astype(F32)
        return both, roll64(both)

    def stack_rows(g, start, rows, a, b):
        low = low_lanes(a.shape[0])
        stack[pl.ds(start, rows), lanes(g)] = jnp.where(low, a, roll64(b)).astype(BF16)
        stack[pl.ds(STACK + start, rows), lanes(g)] = jnp.where(low, roll64(a), b).astype(BF16)

    for part in (KEEP, STACK + KEEP):
        stack[part : part + STACK - KEEP, :] = jnp.zeros((STACK - KEEP, 512), BF16)

    def block(first, other, level):
        rows = pl.ds(pl.multiple_of(first, 16), 16)
        value = []
        for g in range(4):
            theirs = spread(x_ref, g, rows)
            pair = [jnp.where(mine, vis_ref[2 * g + i, rows, :].astype(F32), theirs[i]) for i in range(2)]
            if other is not None:
                near = spread(z_ref, g, other)
                far = spread(xz_ref, g, other)
                pair = [0.5 * (pair[i] + jnp.where(mine, near[i], far[i])) for i in range(2)]
            value.extend(pair)
        result = jones_apply(
            [gl[rows, lanes(c)] for c in range(8)], value, [gr[rows, lanes(c)] for c in range(8)]
        )
        for c in range(8):
            cal[rows, lanes(c)] = result[c].astype(BF16)
        if level == 0:
            for g in range(4):
                stack_rows(g, pl.multiple_of(first, 16), 16, result[2 * g], result[2 * g + 1])

    for level, singles in ((0, 32), (1, 32), (2, 64)):

        def single(i, carry, level=level):
            block(FIRST[level] + i * 16, None, level)
            return carry

        def paired(i, carry, level=level, singles=singles):
            other = pl.ds(pl.multiple_of(level * 64 + i * 16, 16), 16)
            block(FIRST[level] + singles + i * 16, other, level)
            return carry

        lax.fori_loop(0, singles // 16, single, 0, unroll=singles // 16)
        lax.fori_loop(0, 4, paired, 0, unroll=4)

    for u in range(3):
        for c in range(8):
            wide[pl.ds(UNIT_ROW[u] + c, 32, ROWS), :] = cal[u * 32 : (u + 1) * 32, lanes(c)].astype(F32)
    for level in (1, 2):
        packed = 1 << level
        width = 128 >> level
        src = iota((128 * packed, 128), 0)
        mean = jnp.where(
            iota((128 * packed, 128), 1) == (src >> 7) * width + ((src & 127) >> level), 1.0 / packed, 0.0
        ).astype(BF16)
        first = FIRST[level]
        for g in range(8 // packed):
            cols = slice(g * packed * 128, (g + 1) * packed * 128)
            value = dot(cal[first : first + SIZES[level], cols], mean)
            for u in range(SIZES[level] // 32):
                row = UNIT_ROW[first // 32 + u] + g
                wide[pl.ds(row, 32, ROWS), :] = value[u * 32 : (u + 1) * 32]
    for row in range(44, ROWS):
        wide[pl.ds(row, 32, ROWS), :] = jnp.zeros((32, 128), F32)
    for m in range(32):
        out_ref[m, 0:ROWS, :] = wide[m * ROWS : (m + 1) * ROWS, :].astype(BF16)

    for level in (1, 2):
        group = iota((256, 256), 0) >> level == iota((256, 256), 1) >> level
        mean = jnp.where(group, 0.5**level, 0.0).astype(BF16)
        rows = slice(FIRST[level], FIRST[level] + SIZES[level])
        for g in range(4):
            value = dot(cal[rows, g * 256 : (g + 1) * 256], mean)
            stack_rows(g, FIRST[level], SIZES[level], value[:, lanes(0)], value[:, lanes(1)])
    for g in range(0, 4, 2):
        part = dot(weight_ref[...], stack[:, g * 128 : (g + 2) * 128]).astype(BF16)
        for m in range(32):
            for i in range(2):
                row = ROWS + (g + i) * 8
                out_ref[m, row : row + 8, :] = part[m * 8 : (m + 1) * 8, lanes(i)]


def calibrate(me, gains, left, right, weight, vis, x, z, xz):
    vmem = pl.BlockSpec(memory_space=pltpu.VMEM)
    return pl.pallas_call(
        calibrate_kernel,
        in_specs=[pl.BlockSpec(memory_space=pltpu.SMEM)] + [vmem] * 8,
        out_specs=vmem,
        out_shape=jax.ShapeDtypeStruct((32, ROWS + 32, 128), BF16),
        scratch_shapes=[
            pltpu.VMEM((256, 1024), F32),
            pltpu.VMEM((KEEP, 1024), F32),
            pltpu.VMEM((KEEP, 1024), F32),
            pltpu.VMEM((KEEP, 1024), BF16),
            pltpu.VMEM((32 * ROWS, 128), F32),
            pltpu.VMEM((2 * STACK, 512), BF16),
        ],
        compiler_params=pltpu.CompilerParams(vmem_limit_bytes=VMEM_LIMIT),
        name="calibrate",
    )(me, gains, left, right, weight, vis, x, z, xz)


def finish_kernel(recv_ref, pick_ref, lane_ref, time_ref, avg_ref, grid_ref, means):
    for t in range(32):
        means[t, 0:16, :] = recv_ref[t, 0:16, :].astype(F32)
    for side in range(2):
        for r in range(16, ROWS, 8):
            row = r + 32 * side
            level = time_ref[row : row + 8, :]
            at_least = [level >= 2.0, level >= 3.0]
            for x in range(0, 32, 8):
                two = [recv_ref[x + 2 * j + side, r : r + 8, :].astype(F32) for j in range(4)]
                four = [0.5 * (two[2 * j] + two[2 * j + 1]) for j in range(2)]
                eight = 0.5 * (four[0] + four[1])
                top = [jnp.where(at_least[1], eight, four[j]) for j in range(2)]
                for j in range(4):
                    value = jnp.where(at_least[0], top[j // 2], two[j])
                    means[x + 2 * j, row : row + 8, :] = value
                    means[x + 2 * j + 1, row : row + 8, :] = value

    pick = pick_ref[:, 0:MEANS]
    index = [lane_ref[0], lane_ref[1]]
    low = low_lanes(128)

    def step(i, carry):
        first = (i >> 3) * 16 + (i & 7)
        both = jnp.concatenate([means[first], means[first + 8]], axis=1).astype(BF16)
        rows = dot(pick, both)
        for bit in range(2):
            for c in range(8):
                here = slice(c * 16, (c + 1) * 16)
                half = [
                    jnp.take_along_axis(rows[here, lanes(k)], index[bit][here], axis=1, mode="promise_in_bounds")
                    for k in range(2)
                ]
                avg_ref[first + 8 * bit, c] = jnp.where(low[here], half[0], half[1]).astype(BF16)
        return carry

    lax.fori_loop(0, 16, step, 0, unroll=16)

    low8 = low_lanes(8)
    for g in range(4):
        row = ROWS + g * 8
        total = []
        for half in range(2):
            sources = [x * 8 + z for x in (half, half + 2) for z in range(8)]
            value = recv_ref[sources[0], row : row + 8, :].astype(F32)
            for source in sources[1:]:
                value = value + recv_ref[source, row : row + 8, :].astype(F32)
            total.append(value)
        even = jnp.where(low8, total[0], roll64(total[1]))
        odd = jnp.where(low8, roll64(total[0]), total[1])
        for u in range(8):
            grid_ref[u, 2 * g : 2 * g + 1, :] = even[u : u + 1, :]
            grid_ref[u, 2 * g + 1 : 2 * g + 2, :] = odd[u : u + 1, :]


def finish(recv, pick, lane, time):
    vmem = pl.BlockSpec(memory_space=pltpu.VMEM)
    return pl.pallas_call(
        finish_kernel,
        in_specs=[vmem] * 4,
        out_specs=[vmem] * 2,
        out_shape=[
            jax.ShapeDtypeStruct((32, 8, 16, 128), BF16),
            jax.ShapeDtypeStruct((8, 8, 128), F32),
        ],
        scratch_shapes=[pltpu.VMEM((32, MEANS, 128), F32)],
        compiler_params=pltpu.CompilerParams(vmem_limit_bytes=VMEM_LIMIT),
        name="finish",
    )(recv, pick, lane, time)


def shards(visibilities, station_gains, station_pairs, average_bands, tile_map, baseline_order):
    me = lax.axis_index("tm").reshape(1)
    bands = average_bands.T
    hot, position = slots(me, bands, baseline_order[None, :])
    keep, x, z, xz = route(me, hot, visibilities[0])
    x, z, xz = [
        lax.ppermute(value, "tm", [(m, m ^ bits) for m in range(32)]) for value, bits in ((x, 8), (z, 1), (xz, 9))
    ]
    gains = lax.all_to_all(cut_gains(me, station_gains, keep), "chan", 0, 0, tiled=True)
    left, right, weight, pick, lane, time = tables(me, station_pairs.T, bands, tile_map.T, hot, position)
    payload = calibrate(me, gains, left, right, weight, keep, x, z, xz)
    recv = lax.all_to_all(payload, "tm", 0, 0, tiled=True)
    averaged, gridded = finish(recv, pick, lane, time)
    return averaged, gridded


def solution(mesh):
    return jax.shard_map(
        shards,
        mesh=mesh,
        in_specs=(P("tm", None, None, "chan"), P(None, "chan", None), P(), P(), P(), P()),
        out_specs=(P(None, None, "tm", "chan"), P("tm", None, "chan")),
        check_vma=False,
    )
```
